512 devices in a mesh: dom: 128 (over y, z, core), rep: 4 (over x).
Axes of the slice: x: 4, y: 8, z: 8, core: 2. Of those that a mesh axis runs over, the one named last changes fastest.
Arguments:
- features: bfloat16 [32768, 1024], P('dom', 'rep'), may hold values from -6 to 6
- w_self: bfloat16 [1024, 1024], P('rep'), may hold values from -0.1875 to 0.1875
- w_neigh: bfloat16 [1024, 1024], P('rep'), may hold values from -0.1875 to 0.1875
- grad_out: bfloat16 [32768, 1024], P('dom', 'rep'), may hold values from -6 to 6
- mirror_list: int32 [16384, 4], P('dom'), may hold values from 0 to 255, as said below
- mirror_count: int32 [16384], P('dom'), may hold values from 1 to 4, as said below
- tile_dst: int32 [1024], P('dom'), may hold values from 0 to 1
- tile_src: int32 [1024], P('dom'), may hold values from 0 to 5
- tiles: bfloat16 [1024, 128, 128], P('dom'), may hold values from 0 to 4, as said below
Outputs:
- hidden_out: bfloat16 [32768, 1024], P('dom', 'rep')
- grad_features: bfloat16 [32768, 1024], P('dom', 'rep')
- grad_self: bfloat16 [1024, 1024], P('rep')
- grad_neigh: bfloat16 [1024, 1024], P('rep')
The draws below stay inside these ranges and needn't reach their ends.
Inputs may be any that keep to these rules, and one draw needn't show every extreme that they name: `mirror_list`: the entries of one row are distinct. `mirror_count`: every partition has a peer whose count is exactly 4. Weights are zero in columns that fall on unused mirror slots; on each partition the slots after its live tiles hold zeros, and some partition has all 8 slots live.
All inputs are finite; a program needn't handle non-finite values.
Results may differ from the reference program's by a relative error of at most 0.0058.
Values may be sent and summed in bfloat16 or wider, within the bound.
A program may use at most 64 MiB of HBM per device.

```python
import jax
import jax.numpy as jnp
from jax import lax

D = 1024
TILE = 128
V = 256
MIRROR_DEV = 512
TILES = 8
M_PEER = 4
VERTICES = 32768
N_DOM = 128


def count_table(key):
    base = jax.random.fold_in(key, 11)
    counts = jax.random.randint(jax.random.fold_in(base, 1), (N_DOM, N_DOM), 1, M_PEER + 1)
    full_peer = jax.random.randint(jax.random.fold_in(base, 2), (N_DOM,), 0, N_DOM)
    counts = jnp.where(jnp.arange(N_DOM)[None, :] == full_peer[:, None], M_PEER, counts)
    return counts.astype(jnp.int32)


def live_tiles(key):
    base = jax.random.fold_in(key, 31)
    first = jax.random.randint(jax.random.fold_in(base, 1), (N_DOM,), 0, TILES)
    second = jax.random.randint(jax.random.fold_in(base, 2), (N_DOM,), 0, TILES)
    counts = 1 + first * second // TILES
    busiest = jax.random.randint(jax.random.fold_in(base, 3), (), 0, N_DOM)
    counts = jnp.where(jnp.arange(N_DOM) == busiest, TILES, counts)
    return counts.astype(jnp.int32)


def source_tiles(key):
    base = jax.random.fold_in(key, 41)
    return jax.random.randint(base, (N_DOM * TILES,), 0, (V + MIRROR_DEV) // TILE).astype(jnp.int32)


def draw_mirror_count(key, part):
    return count_table(key).reshape(-1)


def draw_mirror_list(key, part):
    base = jax.random.fold_in(key, 23)
    row_keys = jax.random.split(base, N_DOM * N_DOM)
    picked = jax.vmap(lambda row_key: jax.random.permutation(row_key, V)[:M_PEER])(row_keys)
    return picked.astype(jnp.int32)


def draw_tile_dst(key, part):
    base = jax.random.fold_in(key, 53)
    return jax.random.randint(base, (N_DOM * TILES,), 0, V // TILE).astype(jnp.int32)


def draw_tile_src(key, part):
    return source_tiles(key)


def draw_tiles(key, part):
    counts = count_table(key)
    live_count = live_tiles(key)
    src_ids = source_tiles(key).reshape(N_DOM, TILES)
    column = src_ids[:, :, None] * TILE + jnp.arange(TILE)[None, None, :]
    mirror_slot = jnp.maximum(column - V, 0)
    peer_ids = jnp.minimum(mirror_slot // M_PEER, N_DOM - 1)
    slot_ids = mirror_slot % M_PEER
    device_ids = jnp.broadcast_to(jnp.arange(N_DOM)[:, None, None], column.shape)
    count_for = counts[peer_ids, device_ids]
    column_live = (column < V) | (slot_ids < count_for)
    tile_live = jnp.arange(TILES)[None, :] < live_count[:, None]
    base = jax.random.fold_in(key, 67)
    shape = (N_DOM, TILES, TILE, TILE)
    edge_mask = jax.random.randint(jax.random.fold_in(base, 1), shape, 0, 8) == 0
    values = jnp.exp(jax.random.uniform(jax.random.fold_in(base, 2), shape, jnp.float32, jnp.log(0.25), jnp.log(4.0)))
    keep = edge_mask & column_live[:, :, None, :] & tile_live[:, :, None, None]
    result = jnp.where(keep, values, 0.0)
    return result.reshape(N_DOM * TILES, TILE, TILE).astype(jnp.bfloat16)


def levels(stream_key, dims, shards, smallest, high):
    level = 1.0
    for axis_at, parts in shards:
        heights = jax.random.uniform(jax.random.fold_in(jax.random.fold_in(stream_key, 6), axis_at), (parts,), jnp.float32, smallest / len(shards), high / len(shards))
        level = level * jnp.repeat(jnp.exp(heights), dims[axis_at] // parts).reshape((-1,) + (1,) * (len(dims) - 1 - axis_at))
    return level


def gaussian(key, shape, spread, bound, shards=(), kind=jnp.bfloat16):
    values = jax.random.normal(key, shape, jnp.float32) * spread
    if len(shards) > 0:
        values = levels(key, shape, shards, -0.22, 0.18) * values
    return jnp.clip(values, min=-bound, max=bound).astype(kind)


def setup_inputs(seed: int = 0) -> dict:
    arg_keys = jax.random.split(jax.random.key(seed), 10)
    return {
        "features": gaussian(arg_keys[0], (VERTICES, D), 1.0, 6.0, ((0, 128), (1, 4))),
        "w_self": gaussian(arg_keys[1], (D, D), D ** -0.5, 0.1875, ((0, 4),)),
        "w_neigh": gaussian(arg_keys[2], (D, D), D ** -0.5, 0.1875, ((0, 4),)),
        "grad_out": gaussian(arg_keys[3], (VERTICES, D), 1.0, 6.0, ((0, 128), (1, 4))),
        "mirror_list": draw_mirror_list(jax.random.fold_in(arg_keys[9], 71), 0),
        "mirror_count": draw_mirror_count(jax.random.fold_in(arg_keys[9], 71), 0),
        "tile_dst": draw_tile_dst(jax.random.fold_in(arg_keys[9], 71), 0),
        "tile_src": draw_tile_src(jax.random.fold_in(arg_keys[9], 71), 0),
        "tiles": draw_tiles(jax.random.fold_in(arg_keys[9], 71), 0),
    }


def mirror_index(mirror_list, mirror_count, device):
    slot_count = MIRROR_DEV // N_DOM
    peer_lists = mirror_list.reshape(N_DOM, N_DOM, slot_count)[:, device, :]
    counts = mirror_count.reshape(N_DOM, N_DOM)[:, device]
    source_rows = (jnp.arange(N_DOM, dtype=jnp.int32)[:, None] * V + peer_lists).reshape(-1)
    slot_ids = jnp.arange(slot_count, dtype=jnp.int32)
    live_mask = (slot_ids[None, :] < counts[:, None]).reshape(-1)
    return source_rows, live_mask


def reference(features, w_self, w_neigh, grad_out, mirror_list, mirror_count, tile_dst, tile_src, tiles):
    src_count = (V + MIRROR_DEV) // TILE
    dst_count = V // TILE
    highest = lax.Precision.HIGHEST

    def device_tiles(device):
        block = lax.dynamic_slice_in_dim(tiles, device * TILES, TILES, 0).astype(jnp.float32)
        dst_ids = lax.dynamic_slice_in_dim(tile_dst, device * TILES, TILES, 0)
        src_ids = lax.dynamic_slice_in_dim(tile_src, device * TILES, TILES, 0)
        dst_onehot = (dst_ids[None, :] == jnp.arange(dst_count, dtype=jnp.int32)[:, None]).astype(jnp.float32)
        src_onehot = (src_ids[None, :] == jnp.arange(src_count, dtype=jnp.int32)[:, None]).astype(jnp.float32)
        return block, dst_ids, src_ids, dst_onehot, src_onehot

    def forward_one(device):
        source_rows, live_mask = mirror_index(mirror_list, mirror_count, device)
        mirrors = jnp.where(live_mask[:, None], features[source_rows], 0).astype(features.dtype)
        own_rows = lax.dynamic_slice_in_dim(features, device * V, V, 0)
        row_table = jnp.concatenate([own_rows, mirrors], axis=0)
        block, dst_ids, src_ids, dst_onehot, src_onehot = device_tiles(device)
        gathered = row_table.reshape(src_count, TILE, D)[src_ids].astype(jnp.float32)
        contrib = jnp.einsum('tij,tjd->tid', block, gathered, precision=highest)
        summed = jnp.einsum('st,tid->sid', dst_onehot, contrib, precision=highest).reshape(V, D)
        degree = jnp.einsum('st,ti->si', dst_onehot, jnp.sum(block, axis=2), precision=highest).reshape(V)
        aggregated = (summed / jnp.maximum(degree, 1.0)[:, None]).astype(jnp.bfloat16)
        return aggregated, degree

    aggregated, degree = lax.map(forward_one, jnp.arange(N_DOM, dtype=jnp.int32))
    aggregated = aggregated.reshape(VERTICES, D)
    degree = degree.reshape(VERTICES)
    pre_act = jnp.dot(features, w_self, preferred_element_type=jnp.float32) + jnp.dot(aggregated, w_neigh, preferred_element_type=jnp.float32)
    gate_sig = jax.nn.sigmoid(pre_act)
    hidden_out = (pre_act * gate_sig).astype(jnp.bfloat16)
    grad_pre = (grad_out.astype(jnp.float32) * (gate_sig + pre_act * gate_sig * (1.0 - gate_sig))).astype(jnp.bfloat16)
    grad_scale = float(VERTICES) ** -0.5
    grad_self = (jnp.dot(features.T, grad_pre, preferred_element_type=jnp.float32) * grad_scale).astype(jnp.bfloat16)
    grad_neigh = (jnp.dot(aggregated.T, grad_pre, preferred_element_type=jnp.float32) * grad_scale).astype(jnp.bfloat16)
    direct = jnp.dot(grad_pre, w_self.T, preferred_element_type=jnp.float32)
    grad_agg = (jnp.dot(grad_pre, w_neigh.T, preferred_element_type=jnp.float32) / jnp.maximum(degree, 1.0)[:, None]).astype(jnp.bfloat16)

    def backward_one(accum, device):
        block, dst_ids, src_ids, dst_onehot, src_onehot = device_tiles(device)
        grad_dev = lax.dynamic_slice_in_dim(grad_agg, device * V, V, 0)
        grad_tiles = grad_dev.reshape(dst_count, TILE, D)[dst_ids].astype(jnp.float32)
        contrib = jnp.einsum('tij,tid->tjd', block, grad_tiles, precision=highest)
        table_grad = jnp.einsum('st,tjd->sjd', src_onehot, contrib, precision=highest).reshape(src_count * TILE, D)
        own_part = lax.dynamic_slice_in_dim(accum, device * V, V, 0) + table_grad[:V]
        accum = lax.dynamic_update_slice_in_dim(accum, own_part, device * V, 0)
        source_rows, live_mask = mirror_index(mirror_list, mirror_count, device)
        mirror_part = jnp.where(live_mask[:, None], table_grad[V:], jnp.float32(0.0))
        accum = accum.at[source_rows].add(mirror_part)
        return accum, None

    accum, unused = lax.scan(backward_one, jnp.zeros((VERTICES, D), jnp.float32), jnp.arange(N_DOM, dtype=jnp.int32))
    grad_features = (direct + accum).astype(jnp.bfloat16)
    return hidden_out, grad_features, grad_self, grad_neigh
```

```python
import functools

import jax
import jax.numpy as jnp
from jax import lax
from jax.experimental import pallas as pl
from jax.experimental.pallas import tpu as pltpu
from jax.sharding import PartitionSpec as P

MESH = pl.DeviceIdType.MESH
F32 = jnp.float32
BF16 = jnp.bfloat16
CORES = 2
GRIDS = {128: (8, 8), 8: (2, 2)}
CUTS = {8: (2, 4), 2: (1, 2)}

NN = (((1,), (0,)), ((), ()))
TN = (((0,), (0,)), ((), ()))
NT = (((1,), (1,)), ((), ()))


def dot(a, b, dims=NN):
    return lax.dot_general(a, b, dims, preferred_element_type=F32)


class Exchange:
    def __init__(self, n, me, device, src, dst, send_sem, recv_sem):
        self.n, self.me, self.device = n, me, device
        self.src, self.dst = src, dst
        self.send_sem, self.recv_sem = send_sem, recv_sem

    def copy(self, k, src, dst, peer):
        return pltpu.make_async_remote_copy(
            src_ref=src,
            dst_ref=dst,
            send_sem=self.send_sem.at[k - 1],
            recv_sem=self.recv_sem.at[k - 1],
            device_id=self.device(peer),
            device_id_type=MESH,
        )

    def each(self, step):
        if self.n == 2:
            step(1)
        else:
            lax.fori_loop(1, self.n, lambda k, c: (step(k), c)[1], 0)

    def outgoing(self, k):
        peer = lax.rem(self.me + k, self.n)
        return self.copy(k, self.src(peer), self.dst(self.me, k), peer)

    def start(self):
        self.each(lambda k: self.outgoing(k).start())

    def wait_send(self):
        self.each(lambda k: self.outgoing(k).wait_send())

    def wait_recv_one(self, k):
        peer = lax.rem(self.me - k + self.n, self.n)
        slot = self.dst(peer, k)
        self.copy(k, slot, slot, peer).wait_recv()

    def wait_recv(self):
        self.each(self.wait_recv_one)


def kernel(
    dims,
    feat, w_self, w_neigh, grad_out, list_t, count, tile_dst, tile_src, tiles,
    hidden, grad_feat, out_w,
    perm01, perm10, hot0, hot1, edges, degree, table,
    o0, a0, s0, b0, o1, a1, s1, b1,
    part, pre_send, pre_recv, grads, grads_peer, lhs, lhs_peer, direct,
    c0, d0, e0, f0, c1, d1, e1, f1,
    w_acc, wa_send, wa_recv, wb_send, wb_recv, wb_own,
    sem_a, sem_b, sem_c, sem_d, sem_e, sem_f, sem_g, sem_h,
    sem_i, sem_j, sem_k, sem_l, sem_m, sem_n, sem_o, sem_p, sem_q, sem_r, sem_s, sem_t, sem_u,
):
    ny, nz, nx = dims
    ng = nz * CORES
    nd = ny * ng
    rows, width = feat.shape
    half = width // 2
    slots = list_t.shape[0]
    entries = nd * slots
    tile_count, tile_rows = tiles.shape[0], tiles.shape[1]
    dst_count = rows // tile_rows
    src_count = (rows + entries) // tile_rows
    full = nx * width

    dom = lax.axis_index("dom")
    x = lax.axis_index("rep")
    y = lax.div(dom, ng)
    g = lax.rem(dom, ng)
    z = lax.div(g, CORES)
    c = lax.rem(g, CORES)

    def at_g(peer):
        return (y * ng + peer, x)

    def at_y(peer):
        return (peer * ng + g, x)

    def at_z(peer):
        return (y * ng + peer * CORES + c, x)

    def at_c(peer):
        return (y * ng + z * CORES + peer, x)

    def at_x(peer):
        return (dom, peer)

    barrier = pltpu.get_barrier_semaphore()

    def greet(n, me, device):
        def step(k, carry):
            pl.semaphore_signal(
                barrier, inc=1, device_id=device(lax.rem(me + k, n)), device_id_type=MESH
            )
            return carry

        lax.fori_loop(1, n, step, 0)

    greet(ng, g, at_g)
    greet(ny, y, at_y)
    greet(nx, x, at_x)

    def iota(shape, axis):
        return lax.broadcasted_iota(jnp.int32, shape, axis)

    col = iota((1, entries), 1)
    row = iota((entries, entries), 0)

    def selection(index):
        return jnp.where(row == index, 1.0, 0.0).astype(BF16)

    from_listed = selection(lax.rem(col, slots) * nd + lax.div(col, slots))
    y_in = lax.rem(lax.div(col, slots), ny)
    g_in = lax.div(col, slots * ny)
    slot_in = lax.rem(col, slots)
    perm01[...] = selection((y_in * ng + g_in) * slots + slot_in)

    listed = jnp.concatenate(
        [jnp.where(j < count[...], list_t[j : j + 1, :], -1) for j in range(slots)], axis=1
    )
    listed = jnp.broadcast_to(listed.astype(F32), (8, entries)).astype(BF16)
    natural = dot(listed, from_listed)
    transposed = dot(natural.astype(BF16), perm01[...])
    vertex = iota((rows, entries), 0).astype(F32)
    hot0[...] = jnp.where(vertex == transposed[0:1, :], 1.0, 0.0).astype(BF16)
    hot1[...] = jnp.where(vertex == natural[0:1, :], 1.0, 0.0).astype(BF16)
    per_g, per_y = entries // ng, entries // ny
    o0[...] = dot(hot0[...], feat[:, :half], TN).astype(BF16).reshape(ng, per_g, half)
    o1[...] = dot(hot1[...], feat[:, half:], TN).astype(BF16).reshape(ny, per_y, half)

    pl.semaphore_wait(barrier, (ng - 1) + (ny - 1) + (nx - 1))

    out_a0 = Exchange(ng, g, at_g, lambda p: o0.at[p], lambda s, k: a0.at[s], *sem_pair(sem_a))
    out_a1 = Exchange(ny, y, at_y, lambda p: o1.at[p], lambda s, k: a1.at[s], *sem_pair(sem_b))
    out_b0 = Exchange(ny, y, at_y, lambda p: s0.at[p], lambda s, k: b0.at[s], *sem_pair(sem_c))
    out_b1 = Exchange(ng, g, at_g, lambda p: s1.at[p], lambda s, k: b1.at[s], *sem_pair(sem_d))
    out_a0.start()
    out_a1.start()
    a0[g] = o0[g]
    a1[y] = o1[y]

    y_out = lax.div(col, slots * ng)
    g_out = lax.rem(lax.div(col, slots), ng)
    perm10[...] = selection((g_out * ny + y_out) * slots + slot_in)
    table[:rows, :] = feat[...]
    lhs[0] = feat[...]
    part[...] = dot(feat[...], w_self[...])
    block_of = tile_dst[...] * src_count + tile_src[...]
    for d in range(dst_count):
        for s in range(src_count):
            here = jnp.where(block_of == d * src_count + s, 1.0, 0.0)
            total = jnp.zeros((tile_rows, tile_rows), F32)
            for t in range(tile_count):
                total += here[:, t : t + 1] * tiles[t].astype(F32)
            top = total.astype(BF16)
            at = (pl.ds(d * tile_rows, tile_rows), pl.ds(s * tile_rows, tile_rows))
            edges[(0,) + at] = top
            edges[(1,) + at] = (total - top.astype(F32)).astype(BF16)
    ones = jnp.ones((rows + entries, tile_rows), BF16)
    degree[...] = jnp.maximum(dot(edges[0], ones) + dot(edges[1], ones), 1.0)

    out_a0.wait_recv()
    s0[...] = dot(perm01[...], a0[...].reshape(entries, half)).astype(BF16).reshape(ny, per_y, half)
    out_b0.start()
    out_a1.wait_recv()
    s1[...] = dot(perm10[...], a1[...].reshape(entries, half)).astype(BF16).reshape(ng, per_g, half)
    out_b1.start()
    b0[y] = s0[y]
    b1[g] = s1[g]
    out_b0.wait_recv()
    table[rows:, :half] = b0[...].reshape(entries, half)
    out_b1.wait_recv()
    table[rows:, half:] = dot(perm01[...], b1[...].reshape(entries, half)).astype(BF16)

    safe = jnp.concatenate([degree[...]] * (width // tile_rows), axis=1)
    summed = dot(edges[0], table[...]) + dot(edges[1], table[...])
    lhs[1] = (summed / safe).astype(BF16)

    send_lhs = Exchange(
        CORES, c, at_c, lambda p: lhs.at[p], lambda s, k: lhs_peer, *sem_pair(sem_e)
    )
    send_lhs.start()

    for q in range(nx):
        here = pl.ds(q * width, width)
        part[:, here] += dot(lhs[1], w_neigh[:, here])
        pre_send[q] = part[:, here].astype(BF16)
    pre = Exchange(
        nx, x, at_x, lambda p: pre_send.at[p], lambda s, k: pre_recv.at[k - 1], *sem_pair(sem_f)
    )
    pre.start()
    pre_act = part[:, pl.ds(pl.multiple_of(x * width, width), width)]
    pre.wait_recv()
    for k in range(nx - 1):
        pre_act = pre_act + pre_recv[k].astype(F32)
    sig = jax.nn.sigmoid(pre_act)
    hidden[...] = (pre_act * sig).astype(BF16)
    grads[x] = (grad_out[...].astype(F32) * (sig + pre_act * sig * (1.0 - sig))).astype(BF16)

    gather = Exchange(nx, x, at_x, lambda p: grads.at[x], lambda s, k: grads.at[s], *sem_pair(sem_g))
    gather.start()

    def pass_on(q, sem):
        return Exchange(
            CORES, c, at_c, lambda p: grads.at[q], lambda s, k: grads_peer.at[q], *sem_pair(sem)
        )

    passes = [pass_on(x, sem_h)] + [
        pass_on(lax.rem(x - k + nx, nx), sem)
        for k, sem in zip(range(1, nx), (sem_i, sem_j, sem_k))
    ]
    passes[0].start()
    for k in range(1, nx):
        gather.wait_recv_one(k)
        passes[k].start()

    direct[...] = jnp.zeros_like(direct)
    grad_agg = jnp.zeros((rows, width), F32)
    for q in range(nx):
        here = pl.ds(q * width, width)
        direct[...] += dot(grads[q], w_self[:, here], NT)
        grad_agg += dot(grads[q], w_neigh[:, here], NT)
    grad_agg = (grad_agg / safe).astype(BF16)
    table_grad = dot(edges[0], grad_agg, TN) + dot(edges[1], grad_agg, TN)
    direct[...] += table_grad[:rows, :]
    mirror = table_grad[rows:, :].astype(BF16)

    c0[...] = mirror[:, :half].reshape(ny, per_y, half)
    c1[...] = dot(perm10[...], mirror[:, half:]).astype(BF16).reshape(ng, per_g, half)
    back_d0 = Exchange(ny, y, at_y, lambda p: c0.at[p], lambda s, k: d0.at[s], *sem_pair(sem_l))
    back_d1 = Exchange(ng, g, at_g, lambda p: c1.at[p], lambda s, k: d1.at[s], *sem_pair(sem_m))
    back_f0 = Exchange(ng, g, at_g, lambda p: e0.at[p], lambda s, k: f0.at[s], *sem_pair(sem_n))
    back_f1 = Exchange(ny, y, at_y, lambda p: e1.at[p], lambda s, k: f1.at[s], *sem_pair(sem_o))
    back_d0.start()
    back_d1.start()
    d0[y] = c0[y]
    d1[g] = c1[g]

    w_half = full // 2
    ry, rz = width // ny, width // nz
    send_lhs.wait_recv()
    for p in passes:
        p.wait_recv()
    own = lhs[c]
    other = lhs_peer[...]
    for q in range(nx):
        here = pl.ds(q * width, width)
        block = dot(own, grads[q], TN) + dot(other, grads_peer[q], TN)
        w_acc[:, here] = block
        h, at = divmod(q * width, w_half)
        block = block.astype(BF16)
        if h == 0:
            wa_send[0, :, :, pl.ds(at, width)] = block.reshape(ny, ry, width)
        else:
            wa_send[1, :, :, pl.ds(at, width)] = block.reshape(nz, rz, width)

    ways = (
        dict(n=ny, me=y, at=at_y, rows=ry, sem=sem_p),
        dict(n=nz, me=z, at=at_z, rows=rz, sem=sem_q),
    )

    def first(h):
        way = ways[h]
        return Exchange(
            way["n"], way["me"], way["at"],
            lambda p: wa_send.at[h, p], lambda s, k: wa_recv.at[h, k - 1], *sem_pair(way["sem"])
        )

    firsts = [first(0), first(1)]
    for way in firsts:
        way.start()

    back_d0.wait_recv()
    e0[...] = dot(perm10[...], d0[...].reshape(entries, half)).astype(BF16).reshape(ng, per_g, half)
    back_f0.start()
    back_d1.wait_recv()
    e1[...] = dot(perm01[...], d1[...].reshape(entries, half)).astype(BF16).reshape(ny, per_y, half)
    back_f1.start()
    f0[g] = e0[g]
    f1[y] = e1[y]

    def second(h):
        way = ways[1 - h]
        return Exchange(
            way["n"], way["me"], way["at"],
            lambda p: wb_send.at[h, p], lambda s, k: wb_recv.at[h, k - 1],
            *sem_pair((sem_r, sem_s)[h])
        )

    seconds = [second(0), second(1)]
    for h in range(2):
        firsts[h].wait_recv()
        way, after = ways[h], ways[1 - h]
        own_rows = pl.ds(pl.multiple_of(way["me"] * way["rows"], way["rows"]), way["rows"])
        total = w_acc[own_rows, pl.ds(h * w_half, w_half)]
        for k in range(way["n"] - 1):
            total = total + wa_recv[h, k].astype(F32)
        cut_rows, cut_cols = CUTS[after["n"]]
        tr, tc = way["rows"] // cut_rows, w_half // cut_cols
        for i in range(after["n"]):
            r, q = divmod(i, cut_cols)
            piece = total[r * tr : (r + 1) * tr, q * tc : (q + 1) * tc]
            wb_own[h, i] = piece
            wb_send[h, i] = piece.astype(BF16)
        seconds[h].start()

    back_f0.wait_recv()
    grad_feat[:, :half] = (
        direct[:, :half] + dot(hot0[...], f0[...].reshape(entries, half))
    ).astype(BF16)
    back_f1.wait_recv()
    grad_feat[:, half:] = (
        direct[:, half:] + dot(hot1[...], f1[...].reshape(entries, half))
    ).astype(BF16)

    scale = float(rows * nd) ** (-0.5)

    def tile_at(h, i):
        way, after = ways[h], ways[1 - h]
        cut_rows, cut_cols = CUTS[after["n"]]
        tr, tc = way["rows"] // cut_rows, w_half // cut_cols
        r = way["me"] * way["rows"] + lax.div(i, cut_cols) * tr
        q = h * w_half + lax.rem(i, cut_cols) * tc
        return out_w.at[c, pl.ds(pl.multiple_of(r, tr), tr), pl.ds(pl.multiple_of(q, tc), tc)]

    def third(h):
        after = ways[1 - h]
        return Exchange(
            after["n"], after["me"], after["at"],
            lambda p: tile_at(h, after["me"]), lambda s, k: tile_at(h, s),
            *sem_pair((sem_t, sem_u)[h])
        )

    def rows_at(h, i):
        way = ways[h]
        r = pl.multiple_of(i * way["rows"], way["rows"])
        return out_w.at[c, pl.ds(r, way["rows"]), pl.ds(h * w_half, w_half)]

    def fourth(h):
        way = ways[h]
        return Exchange(
            way["n"], way["me"], way["at"],
            lambda p: rows_at(h, way["me"]), lambda s, k: rows_at(h, s),
            *sem_pair(way["sem"], 1)
        )

    thirds, fourths = [third(0), third(1)], [fourth(0), fourth(1)]
    for h in range(2):
        seconds[h].wait_recv()
        after = ways[1 - h]
        total = wb_own[h, after["me"]]
        for k in range(after["n"] - 1):
            total = total + wb_recv[h, k].astype(F32)
        tile_at(h, after["me"])[...] = (total * scale).astype(BF16)
        thirds[h].start()
    for h in range(2):
        thirds[h].wait_recv()
        fourths[h].start()
    for h in range(2):
        fourths[h].wait_recv()
    swap = Exchange(
        CORES, c, at_c, lambda p: out_w.at[c], lambda s, k: out_w.at[s], *sem_pair(sem_e, 1)
    )
    swap.start()
    swap.wait_recv()
    for done in (
        [out_a0, out_a1, out_b0, out_b1, send_lhs, pre, gather, back_d0, back_d1, back_f0, back_f1]
        + passes + firsts + seconds + thirds + fourths + [swap]
    ):
        done.wait_send()


def sem_pair(sems, use=0):
    return sems.at[use, 0], sems.at[use, 1]


def solution(mesh):
    doms, nx = mesh.shape["dom"], mesh.shape["rep"]
    ny, nz = GRIDS[doms]
    ng = nz * CORES

    def local(
        features, w_self, w_neigh, grad_out, mirror_list, mirror_count, tile_dst, tile_src, tiles
    ):
        rows, width = features.shape
        half, full = width // 2, width * nx
        slots = mirror_list.shape[1]
        entries = doms * slots
        tile_rows = tiles.shape[1]
        per_g, per_y = entries // ng, entries // ny
        w_half = full // 2
        assert ny == nz
        block = width // ny
        cut_rows, cut_cols = CUTS[nz]
        tr, tc = block // cut_rows, w_half // cut_cols
        vmem = pl.BlockSpec(memory_space=pltpu.VMEM)

        def scratch(*shape, kind=BF16):
            return pltpu.VMEM(shape, kind)

        def sems(n, uses=1):
            return pltpu.SemaphoreType.DMA((uses, 2, n - 1))

        by_g, by_y = scratch(ng, per_g, half), scratch(ny, per_y, half)
        buffers = [
            scratch(entries, entries), scratch(entries, entries),
            scratch(rows, entries), scratch(rows, entries),
            scratch(2, rows, rows + entries), scratch(rows, tile_rows, kind=F32),
            scratch(rows + entries, width),
            by_g, by_g, by_y, by_y, by_y, by_y, by_g, by_g,
            scratch(rows, full, kind=F32), scratch(nx, rows, width), scratch(nx - 1, rows, width),
            scratch(nx, rows, width), scratch(nx, rows, width),
            scratch(2, rows, width), scratch(rows, width), scratch(rows, width, kind=F32),
            by_y, by_y, by_g, by_g, by_g, by_g, by_y, by_y,
            scratch(width, full, kind=F32),
            scratch(2, ny, block, w_half), scratch(2, ny - 1, block, w_half),
            scratch(2, nz, tr, tc), scratch(2, nz - 1, tr, tc), scratch(2, nz, tr, tc, kind=F32),
        ]
        semaphores = [
            sems(ng), sems(ny), sems(ny), sems(ng),
            sems(2, 2), sems(nx), sems(nx),
            sems(2), sems(2), sems(2), sems(2),
            sems(ny), sems(ng), sems(ng), sems(ny),
            sems(ny, 2), sems(nz, 2), sems(nz), sems(ny), sems(nz), sems(ny),
        ]
        hidden, grad_feat, out_w = pl.pallas_call(
            functools.partial(kernel, (ny, nz, nx)),
            out_shape=(
                jax.ShapeDtypeStruct((rows, width), BF16),
                jax.ShapeDtypeStruct((rows, width), BF16),
                jax.ShapeDtypeStruct((2, width, full), BF16),
            ),
            in_specs=[vmem] * 9,
            out_specs=(vmem, vmem, vmem),
            scratch_shapes=buffers + semaphores,
            compiler_params=pltpu.CompilerParams(
                collective_id=0, has_side_effects=True, vmem_limit_bytes=40 * 2**20
            ),
        )(
            features, w_self, w_neigh, grad_out, mirror_list.T, mirror_count[None, :],
            tile_dst[None, :], tile_src[None, :], tiles,
        )
        return hidden, grad_feat, out_w[0], out_w[1]

    in_specs = (
        P("dom", "rep"),
        P("rep", None),
        P("rep", None),
        P("dom", "rep"),
        P("dom", None),
        P("dom"),
        P("dom"),
        P("dom"),
        P("dom", None, None),
    )
    out_specs = (P("dom", "rep"), P("dom", "rep"), P("rep", None), P("rep", None))
    return jax.shard_map(local, mesh=mesh, in_specs=in_specs, out_specs=out_specs, check_vma=False)
```

```python
import functools

import jax
import jax.numpy as jnp
from jax import lax
from jax.experimental import pallas as pl
from jax.experimental.pallas import tpu as pltpu
from jax.sharding import PartitionSpec as P

MESH = pl.DeviceIdType.MESH
F32 = jnp.float32
BF16 = jnp.bfloat16
CORES = 2
GRIDS = {128: (8, 8), 8: (2, 2)}

NN = (((1,), (0,)), ((), ()))
TN = (((0,), (0,)), ((), ()))
NT = (((1,), (1,)), ((), ()))


def dot(a, b, dims=NN):
    return lax.dot_general(a, b, dims, preferred_element_type=F32)


class Exchange:
    def __init__(self, n, me, device, src, dst, send_sem, recv_sem):
        self.n, self.me, self.device = n, me, device
        self.src, self.dst = src, dst
        self.send_sem, self.recv_sem = send_sem, recv_sem

    def copy(self, k, src, dst, peer):
        return pltpu.make_async_remote_copy(
            src_ref=src,
            dst_ref=dst,
            send_sem=self.send_sem.at[k - 1],
            recv_sem=self.recv_sem.at[k - 1],
            device_id=self.device(peer),
            device_id_type=MESH,
        )

    def each(self, step):
        if self.n == 2:
            step(1)
        else:
            lax.fori_loop(1, self.n, lambda k, c: (step(k), c)[1], 0)

    def outgoing(self, k):
        peer = lax.rem(self.me + k, self.n)
        return self.copy(k, self.src(peer), self.dst(self.me, k), peer)

    def start(self):
        self.each(lambda k: self.outgoing(k).start())

    def wait_send(self):
        self.each(lambda k: self.outgoing(k).wait_send())

    def wait_recv_one(self, k):
        peer = lax.rem(self.me - k + self.n, self.n)
        slot = self.dst(peer, k)
        self.copy(k, slot, slot, peer).wait_recv()

    def wait_recv(self):
        self.each(self.wait_recv_one)


def kernel(
    dims,
    feat_in, w_self_in, w_neigh_in, grad_out_in, list_in, count_in, dst_in, src_in, tiles_in,
    hidden, grad_feat, out_w,
    weights, grad_out, list_t, count, tile_dst, tile_src, tiles,
    perm01, perm10, hot0, hot1, edges, degree, table,
    o0, a0, s0, b0, o1, a1, s1, b1,
    acts, acts_peer, w_cols, pre_act, grads, grads_peer, direct, grad_agg,
    c0, d0, e0, f0, c1, d1, e1, f1,
    w_acc, wa_send, wa_recv, wb_send, wb_recv, wt_send,
    in_sem,
    sem_a0, sem_a1, sem_b0, sem_b1, sem_feat, sem_cols, sem_cols_core, sem_agg, sem_acts,
    sem_gather, sem_pass, sem_d0, sem_d1, sem_f0, sem_f1, sem_first, sem_second,
    sem_third, sem_fourth, sem_swap,
):
    ny, nz, nx = dims
    ng = nz * CORES
    nd = ny * ng
    rows, width = feat_in.shape
    half = width // 2
    slots = list_in.shape[0]
    entries = nd * slots
    tile_count, tile_rows = tiles_in.shape[0], tiles_in.shape[1]
    dst_count = rows // tile_rows
    src_count = (rows + entries) // tile_rows
    parts = nz // nx
    band, piece = half // ny, width // parts

    dom = lax.axis_index("dom")
    x = lax.axis_index("rep")
    y = lax.div(dom, ng)
    g = lax.rem(dom, ng)
    z = lax.div(g, CORES)
    c = lax.rem(g, CORES)

    def at_g(peer):
        return (y * ng + peer, x)

    def at_y(peer):
        return (peer * ng + g, x)

    def at_z(peer):
        return (y * ng + peer * CORES + c, x)

    def at_c(peer):
        return (y * ng + z * CORES + peer, x)

    def at_x(peer):
        return (dom, peer)

    def fetch(i, src, dst):
        return pltpu.make_async_copy(src, dst, in_sem.at[i])

    fetches = [
        fetch(0, list_in, list_t),
        fetch(1, count_in, count),
        fetch(2, feat_in, acts.at[0, x]),
        fetch(3, w_self_in, weights.at[0]),
        fetch(4, w_neigh_in, weights.at[1]),
        fetch(5, dst_in, tile_dst),
        fetch(6, src_in, tile_src),
        fetch(7, tiles_in, tiles),
        fetch(8, grad_out_in, grad_out),
    ]
    for f in fetches:
        f.start()

    barrier = pltpu.get_barrier_semaphore()

    def greet_one(device):
        pl.semaphore_signal(barrier, inc=1, device_id=device, device_id_type=MESH)

    def greet(n, me, device):
        def step(k, carry):
            greet_one(device(lax.rem(me + k, n)))
            return carry

        lax.fori_loop(1, n, step, 0)

    greet(ng, g, at_g)
    greet(ny, y, at_y)
    greet(nx, x, at_x)

    ways = (dict(n=ny, me=y, at=at_y), dict(n=nz, me=z, at=at_z))

    def across(h, i, column):
        return (ways[1 - h]["at"](i)[0], column)

    def senders(h, step):
        def one(k, carry):
            i, column = x * parts + lax.div(k, nx), lax.rem(k, nx)

            @pl.when(jnp.logical_or(i != ways[1 - h]["me"], column != x))
            def _():
                step(k, i, column)

            return carry

        lax.fori_loop(0, parts * nx, one, 0)

    expected = (ng - 1) + (ny - 1) + (nx - 1)
    for h in range(2):
        senders(h, lambda k, i, column: greet_one(across(h, i, column)))
        after = ways[1 - h]
        mine = (lax.div(after["me"], parts) == x).astype(jnp.int32)
        expected = expected + after["n"] - mine

    def iota(shape, axis):
        return lax.broadcasted_iota(jnp.int32, shape, axis)

    col = iota((1, entries), 1)
    row = iota((entries, entries), 0)

    def selection(index):
        return jnp.where(row == index, 1.0, 0.0).astype(BF16)

    from_listed = selection(lax.rem(col, slots) * nd + lax.div(col, slots))
    y_in = lax.rem(lax.div(col, slots), ny)
    g_in = lax.div(col, slots * ny)
    slot_in = lax.rem(col, slots)
    perm01[...] = selection((y_in * ng + g_in) * slots + slot_in)

    fetches[0].wait()
    fetches[1].wait()
    listed = jnp.concatenate(
        [jnp.where(j < count[...], list_t[j : j + 1, :], -1) for j in range(slots)], axis=1
    )
    listed = jnp.broadcast_to(listed.astype(F32), (8, entries)).astype(BF16)
    natural = dot(listed, from_listed)
    transposed = dot(natural.astype(BF16), perm01[...])
    vertex = iota((rows, entries), 0).astype(F32)
    hot0[...] = jnp.where(vertex == transposed[0:1, :], 1.0, 0.0).astype(BF16)
    hot1[...] = jnp.where(vertex == natural[0:1, :], 1.0, 0.0).astype(BF16)
    per_g, per_y = entries // ng, entries // ny
    fetches[2].wait()
    feat = acts[0, x]
    o0[...] = dot(hot0[...], feat[:, :half], TN).astype(BF16).reshape(ng, per_g, half)
    o1[...] = dot(hot1[...], feat[:, half:], TN).astype(BF16).reshape(ny, per_y, half)

    pl.semaphore_wait(barrier, expected)

    out_a0 = Exchange(ng, g, at_g, lambda p: o0.at[p], lambda s, k: a0.at[s], *sem_pair(sem_a0))
    out_a1 = Exchange(ny, y, at_y, lambda p: o1.at[p], lambda s, k: a1.at[s], *sem_pair(sem_a1))
    out_b0 = Exchange(ny, y, at_y, lambda p: s0.at[p], lambda s, k: b0.at[s], *sem_pair(sem_b0))
    out_b1 = Exchange(ng, g, at_g, lambda p: s1.at[p], lambda s, k: b1.at[s], *sem_pair(sem_b1))
    out_a0.start()
    out_a1.start()

    def columns(p):
        return pl.ds(pl.multiple_of(p * width, width), width)

    feats = Exchange(
        nx, x, at_x, lambda p: acts.at[0, x], lambda s, k: acts.at[0, s], *sem_pair(sem_feat)
    )
    cols = Exchange(
        nx, x, at_x, lambda p: weights.at[c, :, columns(p)], lambda s, k: w_cols.at[c, s],
        *sem_pair(sem_cols)
    )
    cols_core = Exchange(
        CORES, c, at_c, lambda p: w_cols.at[c], lambda s, k: w_cols.at[s], *sem_pair(sem_cols_core)
    )
    fetches[3].wait()
    fetches[4].wait()
    cols.start()
    feats.start()
    a0[g] = o0[g]
    a1[y] = o1[y]
    w_cols[c, x] = weights[c, :, columns(x)]
    table[:rows, :] = feat

    y_out = lax.div(col, slots * ng)
    g_out = lax.rem(lax.div(col, slots), ng)
    perm10[...] = selection((g_out * ny + y_out) * slots + slot_in)
    for f in fetches[5:]:
        f.wait()

    out_a0.wait_recv()
    s0[...] = dot(perm01[...], a0[...].reshape(entries, half)).astype(BF16).reshape(ny, per_y, half)
    out_b0.start()
    out_a1.wait_recv()
    s1[...] = dot(perm10[...], a1[...].reshape(entries, half)).astype(BF16).reshape(ng, per_g, half)
    out_b1.start()
    b0[y] = s0[y]
    b1[g] = s1[g]

    block_of = tile_dst[...] * src_count + tile_src[...]
    for i in range(dst_count):
        for j in range(src_count):
            here = jnp.where(block_of == i * src_count + j, 1.0, 0.0)
            total = jnp.zeros((tile_rows, tile_rows), F32)
            for t in range(tile_count):
                total += here[:, t : t + 1] * tiles[t].astype(F32)
            top = total.astype(BF16)
            at = (pl.ds(i * tile_rows, tile_rows), pl.ds(j * tile_rows, tile_rows))
            edges[(0,) + at] = top
            edges[(1,) + at] = (total - top.astype(F32)).astype(BF16)
    ones = jnp.ones((rows + entries, tile_rows), BF16)
    degree[...] = jnp.maximum(dot(edges[0], ones) + dot(edges[1], ones), 1.0)
    cols.wait_recv()
    cols_core.start()

    out_b0.wait_recv()
    table[rows:, :half] = b0[...].reshape(entries, half)
    out_b1.wait_recv()
    table[rows:, half:] = dot(perm01[...], b1[...].reshape(entries, half)).astype(BF16)

    safe = jnp.concatenate([degree[...]] * (width // tile_rows), axis=1)
    summed = dot(edges[0], table[...]) + dot(edges[1], table[...])
    acts[1, x] = (summed / safe).astype(BF16)
    aggs = Exchange(
        nx, x, at_x, lambda p: acts.at[1, x], lambda s, k: acts.at[1, s], *sem_pair(sem_agg)
    )
    aggs.start()

    feats.wait_recv()
    cols_core.wait_recv()
    total = dot(acts[1, x], w_cols[1, x])
    for q in range(nx):
        total += dot(acts[0, q], w_cols[0, q])
    pre_act[...] = total
    for k in range(1, nx):
        q = lax.rem(x - k + nx, nx)
        aggs.wait_recv_one(k)
        pre_act[...] += dot(acts[1, q], w_cols[1, q])
    send_acts = Exchange(
        CORES, c, at_c, lambda p: acts.at[p], lambda s, k: acts_peer, *sem_pair(sem_acts)
    )
    send_acts.start()
    value = pre_act[...]
    sig = jax.nn.sigmoid(value)
    grads[x] = (grad_out[...].astype(F32) * (sig + value * sig * (1.0 - sig))).astype(BF16)

    send_grads = Exchange(
        CORES, c, at_c, lambda p: grads.at[x], lambda s, k: grads_peer, *sem_pair(sem_pass)
    )
    gather = Exchange(
        nx, x, at_x, lambda p: grads.at[x], lambda s, k: grads.at[s], *sem_pair(sem_gather)
    )
    send_grads.start()
    gather.start()
    hidden[...] = (value * sig).astype(BF16)

    for q in range(nx):
        w_acc[q] = dot(acts[c, q], grads[x], TN)
    send_acts.wait_recv()
    send_grads.wait_recv()
    for q in range(nx):
        block = w_acc[q] + dot(acts_peer[q], grads_peer[...], TN)
        w_acc[q] = block
        block = block.astype(BF16)
        for h in range(2):
            wa_send[h, :, q] = block[h * half : (h + 1) * half, :].reshape(ny, band, width)

    def first(h):
        way = ways[h]
        return Exchange(
            way["n"], way["me"], way["at"], lambda p: wa_send.at[h, p],
            lambda s, k: wa_recv.at[h, k - 1], *sem_pair(sem_first, h)
        )

    firsts = [first(0), first(1)]
    for way in firsts:
        way.start()

    direct[...] = dot(grads[x], weights[0, :, columns(x)], NT)
    grad_agg[...] = dot(grads[x], weights[1, :, columns(x)], NT)
    for k in range(1, nx):
        q = lax.rem(x - k + nx, nx)
        gather.wait_recv_one(k)
        direct[...] += dot(grads[q], weights[0, :, columns(q)], NT)
        grad_agg[...] += dot(grads[q], weights[1, :, columns(q)], NT)
    scaled = (grad_agg[...] / safe).astype(BF16)
    table_grad = dot(edges[0], scaled, TN) + dot(edges[1], scaled, TN)
    direct[...] += table_grad[:rows, :]
    mirror = table_grad[rows:, :].astype(BF16)

    c0[...] = mirror[:, :half].reshape(ny, per_y, half)
    c1[...] = dot(perm10[...], mirror[:, half:]).astype(BF16).reshape(ng, per_g, half)
    back_d0 = Exchange(ny, y, at_y, lambda p: c0.at[p], lambda s, k: d0.at[s], *sem_pair(sem_d0))
    back_d1 = Exchange(ng, g, at_g, lambda p: c1.at[p], lambda s, k: d1.at[s], *sem_pair(sem_d1))
    back_f0 = Exchange(ng, g, at_g, lambda p: e0.at[p], lambda s, k: f0.at[s], *sem_pair(sem_f0))
    back_f1 = Exchange(ny, y, at_y, lambda p: e1.at[p], lambda s, k: f1.at[s], *sem_pair(sem_f1))
    back_d0.start()
    back_d1.start()
    d0[y] = c0[y]
    d1[g] = c1[g]

    def second(h):
        way = ways[1 - h]
        return Exchange(
            way["n"], way["me"], way["at"], lambda p: wb_send.at[h, p],
            lambda s, k: wb_recv.at[h, k - 1], *sem_pair(sem_second, h)
        )

    seconds = [second(0), second(1)]
    for h in range(2):
        firsts[h].wait_recv()
        way, after = ways[h], ways[1 - h]
        own_rows = pl.ds(pl.multiple_of(h * half + way["me"] * band, band), band)
        for q in range(nx):
            total = w_acc[q, own_rows, :]
            for k in range(way["n"] - 1):
                total = total + wa_recv[h, k, q].astype(F32)
            for i in range(parts):
                wb_send[h, q * parts + i] = total[:, i * piece : (i + 1) * piece]
        seconds[h].start()

    back_d0.wait_recv()
    e0[...] = dot(perm10[...], d0[...].reshape(entries, half)).astype(BF16).reshape(ng, per_g, half)
    back_f0.start()
    back_d1.wait_recv()
    e1[...] = dot(perm01[...], d1[...].reshape(entries, half)).astype(BF16).reshape(ny, per_y, half)
    back_f1.start()
    f0[g] = e0[g]
    f1[y] = e1[y]

    scale = float(rows * nd) ** (-0.5)

    def piece_at(h, i, column):
        r = h * half + ways[h]["me"] * band
        q = column * width + lax.rem(i, parts) * piece
        return out_w.at[c, pl.ds(pl.multiple_of(r, band), band), pl.ds(pl.multiple_of(q, piece), piece)]

    def third(h, k, dst, device, slot):
        return pltpu.make_async_remote_copy(
            src_ref=wt_send.at[h], dst_ref=dst, send_sem=sem_third.at[h, 0, k],
            recv_sem=sem_third.at[h, 1, slot], device_id=device, device_id_type=MESH,
        )

    def thirds(h, step):
        after = ways[1 - h]
        me = after["me"]
        slot = lax.rem(me, parts) * nx + x
        target = lax.div(me, parts)

        def one(k, carry):
            copy = third(h, k, piece_at(h, me, x), across(h, lax.rem(me + k, after["n"]), target), slot)

            @pl.when(jnp.logical_or(k != 0, target != x))
            def _():
                step(copy)

            return carry

        lax.fori_loop(0, after["n"], one, 0)

    for h in range(2):
        seconds[h].wait_recv()
        after = ways[1 - h]
        total = wb_send[h, after["me"]]
        for k in range(after["n"] - 1):
            total = total + wb_recv[h, k]
        wt_send[h] = (total * scale).astype(BF16)
        thirds(h, lambda copy: copy.start())

        @pl.when(lax.div(after["me"], parts) == x)
        def _():
            piece_at(h, after["me"], x)[...] = wt_send[h]

    def band_at(h, i, core):
        return out_w.at[core, pl.ds(pl.multiple_of(h * half + i * band, band), band), :]

    def fourth(h):
        way = ways[h]
        return Exchange(
            way["n"], way["me"], way["at"], lambda p: band_at(h, way["me"], c),
            lambda s, k: band_at(h, s, c), *sem_pair(sem_fourth, h)
        )

    def swap(h, k):
        way = ways[h]
        i = lax.rem(way["me"] - k + way["n"], way["n"])
        return pltpu.make_async_remote_copy(
            src_ref=band_at(h, i, c), dst_ref=band_at(h, i, c), send_sem=sem_swap.at[h, 0, k],
            recv_sem=sem_swap.at[h, 1, k], device_id=at_c(1 - c), device_id_type=MESH,
        )

    fourths = [fourth(0), fourth(1)]
    for h in range(2):
        senders(
            h,
            lambda k, i, column: third(h, 0, piece_at(h, i, column), across(h, i, column), k).wait_recv(),
        )
        fourths[h].start()
        swap(h, 0).start()

    back_f0.wait_recv()
    grad_feat[:, :half] = (
        direct[:, :half] + dot(hot0[...], f0[...].reshape(entries, half))
    ).astype(BF16)
    back_f1.wait_recv()
    grad_feat[:, half:] = (
        direct[:, half:] + dot(hot1[...], f1[...].reshape(entries, half))
    ).astype(BF16)

    def pass_on(k):
        for h in range(2):
            fourths[h].wait_recv_one(k)
            swap(h, k).start()

    fourths[0].each(pass_on)

    def swapped(k, carry):
        for h in range(2):
            swap(h, k).wait_recv()
            swap(h, k).wait_send()
        return carry

    lax.fori_loop(0, ny, swapped, 0)
    for h in range(2):
        thirds(h, lambda copy: copy.wait_send())
    for done in (
        [out_a0, out_a1, out_b0, out_b1, feats, cols, cols_core, aggs, send_acts, send_grads]
        + [gather, back_d0, back_d1, back_f0, back_f1] + firsts + seconds + fourths
    ):
        done.wait_send()


def write_out(hidden, grad_feat, both, out0, out1, out2, out3, sem):
    pairs = ((hidden, out0), (grad_feat, out1), (both.at[0], out2), (both.at[1], out3))
    copies = [pltpu.make_async_copy(src, dst, sem.at[i]) for i, (src, dst) in enumerate(pairs)]
    for copy in copies:
        copy.start()
    for copy in copies:
        copy.wait()


def sem_pair(sems, use=0):
    return sems.at[use, 0], sems.at[use, 1]


def solution(mesh):
    doms, nx = mesh.shape["dom"], mesh.shape["rep"]
    ny, nz = GRIDS[doms]
    ng = nz * CORES

    def local(
        features, w_self, w_neigh, grad_out, mirror_list, mirror_count, tile_dst, tile_src, tiles
    ):
        rows, width = features.shape
        half, full = width // 2, width * nx
        slots = mirror_list.shape[1]
        entries = doms * slots
        tile_count, tile_rows = tiles.shape[0], tiles.shape[1]
        per_g, per_y = entries // ng, entries // ny
        assert ny == nz and rows == width and nz % nx == 0
        parts = nz // nx
        band, piece = half // ny, width // parts
        vmem, stay = (pl.BlockSpec(memory_space=s) for s in (pltpu.VMEM, pl.ANY))

        def scratch(*shape, kind=BF16):
            return pltpu.VMEM(shape, kind)

        def sems(n, uses=1):
            return pltpu.SemaphoreType.DMA((uses, 2, n))

        by_g, by_y = scratch(ng, per_g, half), scratch(ny, per_y, half)
        buffers = [
            scratch(2, width, full), scratch(rows, width),
            scratch(slots, doms, kind=jnp.int32), scratch(1, doms, kind=jnp.int32),
            scratch(1, tile_count, kind=jnp.int32), scratch(1, tile_count, kind=jnp.int32),
            scratch(tile_count, tile_rows, tile_rows),
            scratch(entries, entries), scratch(entries, entries),
            scratch(rows, entries), scratch(rows, entries),
            scratch(2, rows, rows + entries), scratch(rows, tile_rows, kind=F32),
            scratch(rows + entries, width),
            by_g, by_g, by_y, by_y, by_y, by_y, by_g, by_g,
            scratch(2, nx, rows, width), scratch(nx, rows, width), scratch(2, nx, width, width),
            scratch(rows, width, kind=F32), scratch(nx, rows, width), scratch(rows, width),
            scratch(rows, width, kind=F32), scratch(rows, width, kind=F32),
            by_y, by_y, by_g, by_g, by_g, by_g, by_y, by_y,
            scratch(nx, width, width, kind=F32),
            scratch(2, ny, nx, band, width), scratch(2, ny - 1, nx, band, width),
            scratch(2, nz, band, piece, kind=F32), scratch(2, nz - 1, band, piece, kind=F32),
            scratch(2, band, piece),
        ]
        semaphores = [
            pltpu.SemaphoreType.DMA((9,)),
            sems(ng - 1), sems(ny - 1), sems(ny - 1), sems(ng - 1),
            sems(nx - 1), sems(nx - 1), sems(1), sems(nx - 1), sems(1),
            sems(nx - 1), sems(1), sems(ny - 1), sems(ng - 1), sems(ng - 1), sems(ny - 1),
            sems(ny - 1, 2), sems(ny - 1, 2), sems(nz, 2), sems(ny - 1, 2), sems(ny, 2),
        ]
        shapes = (
            jax.ShapeDtypeStruct((rows, width), BF16),
            jax.ShapeDtypeStruct((rows, width), BF16),
            jax.ShapeDtypeStruct((2, width, full), BF16),
        )
        results = pl.pallas_call(
            functools.partial(kernel, (ny, nz, nx)),
            out_shape=shapes,
            in_specs=[pl.BlockSpec(memory_space=pltpu.HBM)] * 9,
            out_specs=(vmem, vmem, vmem),
            scratch_shapes=buffers + semaphores,
            compiler_params=pltpu.CompilerParams(
                collective_id=0, has_side_effects=True, vmem_limit_bytes=62 * 2**20
            ),
        )(
            features, w_self, w_neigh, grad_out, mirror_list.T, mirror_count[None, :],
            tile_dst[None, :], tile_src[None, :], tiles,
        )
        weight = jax.ShapeDtypeStruct((width, full), BF16)
        return pl.pallas_call(
            write_out,
            out_shape=shapes[:2] + (weight, weight),
            in_specs=[stay] * 3,
            out_specs=(stay,) * 4,
            scratch_shapes=[pltpu.SemaphoreType.DMA((4,))],
        )(*results)

    in_specs = (
        P("dom", "rep"),
        P("rep", None),
        P("rep", None),
        P("dom", "rep"),
        P("dom", None),
        P("dom"),
        P("dom"),
        P("dom"),
        P("dom", None, None),
    )
    out_specs = (P("dom", "rep"), P("dom", "rep"), P("rep", None), P("rep", None))
    return jax.shard_map(local, mesh=mesh, in_specs=in_specs, out_specs=out_specs, check_vma=False)
```

```python
import functools

import jax
import jax.numpy as jnp
from jax import lax
from jax.experimental import pallas as pl
from jax.experimental.pallas import tpu as pltpu
from jax.sharding import PartitionSpec as P

MESH = pl.DeviceIdType.MESH
F32 = jnp.float32
BF16 = jnp.bfloat16
CORES = 2
GRIDS = {128: (8, 8), 8: (2, 2)}

NN = (((1,), (0,)), ((), ()))
TN = (((0,), (0,)), ((), ()))
NT = (((1,), (1,)), ((), ()))


def dot(a, b, dims=NN):
    return lax.dot_general(a, b, dims, preferred_element_type=F32)


class Exchange:
    def __init__(self, n, me, device, src, dst, send_sem, recv_sem):
        self.n, self.me, self.device = n, me, device
        self.src, self.dst = src, dst
        self.send_sem, self.recv_sem = send_sem, recv_sem

    def copy(self, k, src, dst, peer):
        return pltpu.make_async_remote_copy(
            src_ref=src,
            dst_ref=dst,
            send_sem=self.send_sem.at[k - 1],
            recv_sem=self.recv_sem.at[k - 1],
            device_id=self.device(peer),
            device_id_type=MESH,
        )

    def each(self, step):
        if self.n == 2:
            step(1)
        else:
            lax.fori_loop(1, self.n, lambda k, c: (step(k), c)[1], 0)

    def outgoing(self, k):
        peer = lax.rem(self.me + k, self.n)
        return self.copy(k, self.src(peer), self.dst(self.me, k), peer)

    def start(self):
        self.each(lambda k: self.outgoing(k).start())

    def wait_send(self):
        self.each(lambda k: self.outgoing(k).wait_send())

    def wait_recv_one(self, k):
        peer = lax.rem(self.me - k + self.n, self.n)
        slot = self.dst(peer, k)
        self.copy(k, slot, slot, peer).wait_recv()

    def wait_recv(self):
        self.each(self.wait_recv_one)


def kernel(
    dims,
    feat_in, w_self_in, w_neigh_in, grad_out_in, list_in, count_in, dst_in, src_in, tiles_in,
    hidden, grad_feat, out_w,
    weights, grad_out, list_t, count, tile_dst, tile_src, tiles,
    perm01, perm10, hot0, hot1, edges, degree, table,
    o0, a0, s0, b0, o1, a1, s1, b1,
    acts, acts_peer, w_cols, pre_act, grads, grads_peer, direct, grad_agg,
    c0, d0, e0, f0, c1, d1, e1, f1,
    w_acc, wa_send, wa_recv, wb_send, wb_recv, wt_send,
    in_sem,
    sem_a0, sem_a1, sem_b0, sem_b1, sem_feat, sem_cols, sem_cols_core, sem_agg, sem_acts,
    sem_gather, sem_pass, sem_d0, sem_d1, sem_f0, sem_f1, sem_first, sem_second,
    sem_third, sem_fourth, sem_swap,
):
    ny, nz, nx = dims
    ng = nz * CORES
    nd = ny * ng
    rows, width = feat_in.shape
    half = width // 2
    slots = list_in.shape[0]
    entries = nd * slots
    tile_count, tile_rows = tiles_in.shape[0], tiles_in.shape[1]
    dst_count = rows // tile_rows
    src_count = (rows + entries) // tile_rows
    parts = nz // nx
    band, piece = half // ny, width // parts

    dom = lax.axis_index("dom")
    x = lax.axis_index("rep")
    y = lax.div(dom, ng)
    g = lax.rem(dom, ng)
    z = lax.div(g, CORES)
    c = lax.rem(g, CORES)

    def at_g(peer):
        return (y * ng + peer, x)

    def at_y(peer):
        return (peer * ng + g, x)

    def at_z(peer):
        return (y * ng + peer * CORES + c, x)

    def at_c(peer):
        return (y * ng + z * CORES + peer, x)

    def at_x(peer):
        return (dom, peer)

    def fetch(i, src, dst):
        return pltpu.make_async_copy(src, dst, in_sem.at[i])

    fetches = [
        fetch(0, list_in, list_t),
        fetch(1, count_in, count),
        fetch(2, feat_in, acts.at[0, x]),
        fetch(3, w_self_in, weights.at[0]),
        fetch(4, w_neigh_in, weights.at[1]),
        fetch(5, dst_in, tile_dst),
        fetch(6, src_in, tile_src),
        fetch(7, tiles_in, tiles),
        fetch(8, grad_out_in, grad_out),
    ]
    for f in fetches:
        f.start()

    barrier = pltpu.get_barrier_semaphore()

    def greet_one(device):
        pl.semaphore_signal(barrier, inc=1, device_id=device, device_id_type=MESH)

    def greet(n, me, device):
        def step(k, carry):
            greet_one(device(lax.rem(me + k, n)))
            return carry

        lax.fori_loop(1, n, step, 0)

    greet(ng, g, at_g)
    greet(ny, y, at_y)
    greet(nx, x, at_x)

    ways = (dict(n=ny, me=y, at=at_y), dict(n=nz, me=z, at=at_z))

    def across(h, i, column):
        return (ways[1 - h]["at"](i)[0], column)

    def senders(h, step):
        def one(k, carry):
            i, column = x * parts + lax.div(k, nx), lax.rem(k, nx)

            @pl.when(jnp.logical_or(i != ways[1 - h]["me"], column != x))
            def _():
                step(k, i, column)

            return carry

        lax.fori_loop(0, parts * nx, one, 0)

    expected = (ng - 1) + (ny - 1) + (nx - 1)
    for h in range(2):
        senders(h, lambda k, i, column: greet_one(across(h, i, column)))
        after = ways[1 - h]
        mine = (lax.div(after["me"], parts) == x).astype(jnp.int32)
        expected = expected + after["n"] - mine

    def iota(shape, axis):
        return lax.broadcasted_iota(jnp.int32, shape, axis)

    col = iota((1, entries), 1)
    row = iota((entries, entries), 0)

    def selection(index):
        return jnp.where(row == index, 1.0, 0.0).astype(BF16)

    from_listed = selection(lax.rem(col, slots) * nd + lax.div(col, slots))
    y_in = lax.rem(lax.div(col, slots), ny)
    g_in = lax.div(col, slots * ny)
    slot_in = lax.rem(col, slots)
    perm01[...] = selection((y_in * ng + g_in) * slots + slot_in)

    fetches[0].wait()
    fetches[1].wait()
    listed = jnp.concatenate(
        [jnp.where(j < count[...], list_t[j : j + 1, :], -1) for j in range(slots)], axis=1
    )
    listed = jnp.broadcast_to(listed.astype(F32), (8, entries)).astype(BF16)
    natural = dot(listed, from_listed)
    transposed = dot(natural.astype(BF16), perm01[...])
    vertex = iota((rows, entries), 0).astype(F32)
    hot0[...] = jnp.where(vertex == transposed[0:1, :], 1.0, 0.0).astype(BF16)
    hot1[...] = jnp.where(vertex == natural[0:1, :], 1.0, 0.0).astype(BF16)
    per_g, per_y = entries // ng, entries // ny
    fetches[2].wait()
    feat = acts[0, x]
    o0[...] = dot(hot0[...], feat[:, :half], TN).astype(BF16).reshape(ng, per_g, half)
    o1[...] = dot(hot1[...], feat[:, half:], TN).astype(BF16).reshape(ny, per_y, half)

    pl.semaphore_wait(barrier, expected)

    out_a0 = Exchange(ng, g, at_g, lambda p: o0.at[p], lambda s, k: a0.at[s], *sem_pair(sem_a0))
    out_a1 = Exchange(ny, y, at_y, lambda p: o1.at[p], lambda s, k: a1.at[s], *sem_pair(sem_a1))
    out_b0 = Exchange(ny, y, at_y, lambda p: s0.at[p], lambda s, k: b0.at[s], *sem_pair(sem_b0))
    out_b1 = Exchange(ng, g, at_g, lambda p: s1.at[p], lambda s, k: b1.at[s], *sem_pair(sem_b1))
    out_a0.start()
    out_a1.start()

    def columns(p):
        return pl.ds(pl.multiple_of(p * width, width), width)

    feats = Exchange(
        nx, x, at_x, lambda p: acts.at[0, x], lambda s, k: acts.at[0, s], *sem_pair(sem_feat)
    )
    cols = Exchange(
        nx, x, at_x, lambda p: weights.at[c, :, columns(p)], lambda s, k: w_cols.at[c, s],
        *sem_pair(sem_cols)
    )
    cols_core = Exchange(
        CORES, c, at_c, lambda p: w_cols.at[c], lambda s, k: w_cols.at[s], *sem_pair(sem_cols_core)
    )
    fetches[3].wait()
    fetches[4].wait()
    cols.start()
    feats.start()
    a0[g] = o0[g]
    a1[y] = o1[y]
    w_cols[c, x] = weights[c, :, columns(x)]
    table[:rows, :] = feat

    y_out = lax.div(col, slots * ng)
    g_out = lax.rem(lax.div(col, slots), ng)
    perm10[...] = selection((g_out * ny + y_out) * slots + slot_in)
    for f in fetches[5:]:
        f.wait()

    out_a0.wait_recv()
    s0[...] = dot(perm01[...], a0[...].reshape(entries, half)).astype(BF16).reshape(ny, per_y, half)
    out_b0.start()
    out_a1.wait_recv()
    s1[...] = dot(perm10[...], a1[...].reshape(entries, half)).astype(BF16).reshape(ng, per_g, half)
    out_b1.start()
    b0[y] = s0[y]
    b1[g] = s1[g]

    block_of = tile_dst[...] * src_count + tile_src[...]
    for i in range(dst_count):
        for j in range(src_count):
            here = jnp.where(block_of == i * src_count + j, 1.0, 0.0)
            total = jnp.zeros((tile_rows, tile_rows), F32)
            for t in range(tile_count):
                total += here[:, t : t + 1] * tiles[t].astype(F32)
            top = total.astype(BF16)
            at = (pl.ds(i * tile_rows, tile_rows), pl.ds(j * tile_rows, tile_rows))
            edges[(0,) + at] = top
            edges[(1,) + at] = (total - top.astype(F32)).astype(BF16)
    ones = jnp.ones((rows + entries, tile_rows), BF16)
    degree[...] = jnp.maximum(dot(edges[0], ones) + dot(edges[1], ones), 1.0)
    cols.wait_recv()
    cols_core.start()

    out_b0.wait_recv()
    table[rows:, :half] = b0[...].reshape(entries, half)
    out_b1.wait_recv()
    table[rows:, half:] = dot(perm01[...], b1[...].reshape(entries, half)).astype(BF16)

    safe = jnp.concatenate([degree[...]] * (width // tile_rows), axis=1)
    summed = dot(edges[0], table[...]) + dot(edges[1], table[...])
    acts[1, x] = (summed / safe).astype(BF16)
    aggs = Exchange(
        nx, x, at_x, lambda p: acts.at[1, x], lambda s, k: acts.at[1, s], *sem_pair(sem_agg)
    )
    aggs.start()

    feats.wait_recv()
    cols_core.wait_recv()
    total = dot(acts[1, x], w_cols[1, x])
    for q in range(nx):
        total += dot(acts[0, q], w_cols[0, q])
    pre_act[...] = total
    for k in range(1, nx):
        q = lax.rem(x - k + nx, nx)
        aggs.wait_recv_one(k)
        pre_act[...] += dot(acts[1, q], w_cols[1, q])
    send_acts = Exchange(
        CORES, c, at_c, lambda p: acts.at[p], lambda s, k: acts_peer, *sem_pair(sem_acts)
    )
    send_acts.start()
    value = pre_act[...]
    sig = jax.nn.sigmoid(value)
    grads[x] = (grad_out[...].astype(F32) * (sig + value * sig * (1.0 - sig))).astype(BF16)

    send_grads = Exchange(
        CORES, c, at_c, lambda p: grads.at[x], lambda s, k: grads_peer, *sem_pair(sem_pass)
    )
    gather = Exchange(
        nx, x, at_x, lambda p: grads.at[x], lambda s, k: grads.at[s], *sem_pair(sem_gather)
    )
    send_grads.start()
    gather.start()
    hidden[...] = (value * sig).astype(BF16)

    for q in range(nx):
        w_acc[q] = dot(acts[c, q], grads[x], TN)
    send_acts.wait_recv()
    send_grads.wait_recv()
    for q in range(nx):
        block = w_acc[q] + dot(acts_peer[q], grads_peer[...], TN)
        w_acc[q] = block
        block = block.astype(BF16)
        for h in range(2):
            wa_send[h, :, q] = block[h * half : (h + 1) * half, :].reshape(ny, band, width)

    def first(h):
        way = ways[h]
        return Exchange(
            way["n"], way["me"], way["at"], lambda p: wa_send.at[h, p],
            lambda s, k: wa_recv.at[h, k - 1], *sem_pair(sem_first, h)
        )

    firsts = [first(0), first(1)]
    for way in firsts:
        way.start()

    direct[...] = dot(grads[x], weights[0, :, columns(x)], NT)
    grad_agg[...] = dot(grads[x], weights[1, :, columns(x)], NT)
    for k in range(1, nx):
        q = lax.rem(x - k + nx, nx)
        gather.wait_recv_one(k)
        direct[...] += dot(grads[q], weights[0, :, columns(q)], NT)
        grad_agg[...] += dot(grads[q], weights[1, :, columns(q)], NT)
    scaled = (grad_agg[...] / safe).astype(BF16)
    table_grad = dot(edges[0], scaled, TN) + dot(edges[1], scaled, TN)
    direct[...] += table_grad[:rows, :]
    mirror = table_grad[rows:, :].astype(BF16)

    c0[...] = mirror[:, :half].reshape(ny, per_y, half)
    c1[...] = dot(perm10[...], mirror[:, half:]).astype(BF16).reshape(ng, per_g, half)
    back_d0 = Exchange(ny, y, at_y, lambda p: c0.at[p], lambda s, k: d0.at[s], *sem_pair(sem_d0))
    back_d1 = Exchange(ng, g, at_g, lambda p: c1.at[p], lambda s, k: d1.at[s], *sem_pair(sem_d1))
    back_f0 = Exchange(ng, g, at_g, lambda p: e0.at[p], lambda s, k: f0.at[s], *sem_pair(sem_f0))
    back_f1 = Exchange(ny, y, at_y, lambda p: e1.at[p], lambda s, k: f1.at[s], *sem_pair(sem_f1))
    back_d0.start()
    back_d1.start()
    d0[y] = c0[y]
    d1[g] = c1[g]

    def second(h):
        way = ways[1 - h]
        return Exchange(
            way["n"], way["me"], way["at"], lambda p: wb_send.at[h, p],
            lambda s, k: wb_recv.at[h, k - 1], *sem_pair(sem_second, h)
        )

    seconds = [second(0), second(1)]
    for h in range(2):
        firsts[h].wait_recv()
        way, after = ways[h], ways[1 - h]
        own_rows = pl.ds(pl.multiple_of(h * half + way["me"] * band, band), band)
        for q in range(nx):
            total = w_acc[q, own_rows, :]
            for k in range(way["n"] - 1):
                total = total + wa_recv[h, k, q].astype(F32)
            for i in range(parts):
                wb_send[h, q * parts + i] = total[:, i * piece : (i + 1) * piece]
        seconds[h].start()

    back_d0.wait_recv()
    e0[...] = dot(perm10[...], d0[...].reshape(entries, half)).astype(BF16).reshape(ng, per_g, half)
    back_f0.start()
    back_d1.wait_recv()
    e1[...] = dot(perm01[...], d1[...].reshape(entries, half)).astype(BF16).reshape(ny, per_y, half)
    back_f1.start()
    f0[g] = e0[g]
    f1[y] = e1[y]

    scale = float(rows * nd) ** (-0.5)

    def piece_at(h, i, column):
        r = h * half + ways[h]["me"] * band
        q = column * width + lax.rem(i, parts) * piece
        return out_w.at[c, pl.ds(pl.multiple_of(r, band), band), pl.ds(pl.multiple_of(q, piece), piece)]

    def third(h, k, dst, device, slot):
        return pltpu.make_async_remote_copy(
            src_ref=wt_send.at[h], dst_ref=dst, send_sem=sem_third.at[h, 0, k],
            recv_sem=sem_third.at[h, 1, slot], device_id=device, device_id_type=MESH,
        )

    def thirds(h, step):
        after = ways[1 - h]
        me = after["me"]
        slot = lax.rem(me, parts) * nx + x
        target = lax.div(me, parts)

        def one(k, carry):
            copy = third(h, k, piece_at(h, me, x), across(h, lax.rem(me + k, after["n"]), target), slot)

            @pl.when(jnp.logical_or(k != 0, target != x))
            def _():
                step(copy)

            return carry

        lax.fori_loop(0, after["n"], one, 0)

    for h in range(2):
        seconds[h].wait_recv()
        after = ways[1 - h]
        total = wb_send[h, after["me"]]
        for k in range(after["n"] - 1):
            total = total + wb_recv[h, k]
        wt_send[h] = (total * scale).astype(BF16)
        thirds(h, lambda copy: copy.start())

        @pl.when(lax.div(after["me"], parts) == x)
        def _():
            piece_at(h, after["me"], x)[...] = wt_send[h]

    def band_at(h, i, core):
        return out_w.at[core, pl.ds(pl.multiple_of(h * half + i * band, band), band), :]

    def fourth(h):
        way = ways[h]
        return Exchange(
            way["n"], way["me"], way["at"], lambda p: band_at(h, way["me"], c),
            lambda s, k: band_at(h, s, c), *sem_pair(sem_fourth, h)
        )

    def swap(h, k):
        way = ways[h]
        i = lax.rem(way["me"] - k + way["n"], way["n"])
        return pltpu.make_async_remote_copy(
            src_ref=band_at(h, i, c), dst_ref=band_at(h, i, c), send_sem=sem_swap.at[h, 0, k],
            recv_sem=sem_swap.at[h, 1, k], device_id=at_c(1 - c), device_id_type=MESH,
        )

    fourths = [fourth(0), fourth(1)]
    for h in range(2):
        senders(
            h,
            lambda k, i, column: third(h, 0, piece_at(h, i, column), across(h, i, column), k).wait_recv(),
        )
        fourths[h].start()
        swap(h, 0).start()

    back_f0.wait_recv()
    grad_feat[:, :half] = (
        direct[:, :half] + dot(hot0[...], f0[...].reshape(entries, half))
    ).astype(BF16)
    back_f1.wait_recv()
    grad_feat[:, half:] = (
        direct[:, half:] + dot(hot1[...], f1[...].reshape(entries, half))
    ).astype(BF16)

    def pass_on(k):
        for h in range(2):
            fourths[h].wait_recv_one(k)
            swap(h, k).start()

    fourths[0].each(pass_on)

    def swapped(k, carry):
        for h in range(2):
            swap(h, k).wait_recv()
            swap(h, k).wait_send()
        return carry

    lax.fori_loop(0, ny, swapped, 0)
    for h in range(2):
        thirds(h, lambda copy: copy.wait_send())
    for done in (
        [out_a0, out_a1, out_b0, out_b1, feats, cols, cols_core, aggs, send_acts, send_grads]
        + [gather, back_d0, back_d1, back_f0, back_f1] + firsts + seconds + fourths
    ):
        done.wait_send()


def write_out(hidden, grad_feat, both, out0, out1, out2, out3, sem):
    pairs = ((hidden, out0), (grad_feat, out1), (both.at[0], out2), (both.at[1], out3))
    copies = [pltpu.make_async_copy(src, dst, sem.at[i]) for i, (src, dst) in enumerate(pairs)]
    for copy in copies:
        copy.start()
    for copy in copies:
        copy.wait()


def sem_pair(sems, use=0):
    return sems.at[use, 0], sems.at[use, 1]


def solution(mesh):
    doms, nx = mesh.shape["dom"], mesh.shape["rep"]
    ny, nz = GRIDS[doms]
    ng = nz * CORES

    def local(
        features, w_self, w_neigh, grad_out, mirror_list, mirror_count, tile_dst, tile_src, tiles
    ):
        rows, width = features.shape
        half, full = width // 2, width * nx
        slots = mirror_list.shape[1]
        entries = doms * slots
        tile_count, tile_rows = tiles.shape[0], tiles.shape[1]
        per_g, per_y = entries // ng, entries // ny
        assert ny == nz and rows == width and nz % nx == 0
        parts = nz // nx
        band, piece = half // ny, width // parts
        vmem, stay = (pl.BlockSpec(memory_space=s) for s in (pltpu.VMEM, pl.ANY))

        def scratch(*shape, kind=BF16):
            return pltpu.VMEM(shape, kind)

        def sems(n, uses=1):
            return pltpu.SemaphoreType.DMA((uses, 2, n))

        by_g, by_y = scratch(ng, per_g, half), scratch(ny, per_y, half)
        buffers = [
            scratch(2, width, full), scratch(rows, width),
            scratch(slots, doms, kind=jnp.int32), scratch(1, doms, kind=jnp.int32),
            scratch(1, tile_count, kind=jnp.int32), scratch(1, tile_count, kind=jnp.int32),
            scratch(tile_count, tile_rows, tile_rows),
            scratch(entries, entries), scratch(entries, entries),
            scratch(rows, entries), scratch(rows, entries),
            scratch(2, rows, rows + entries), scratch(rows, tile_rows, kind=F32),
            scratch(rows + entries, width),
            by_g, by_g, by_y, by_y, by_y, by_y, by_g, by_g,
            scratch(2, nx, rows, width), scratch(nx, rows, width), scratch(2, nx, width, width),
            scratch(rows, width, kind=F32), scratch(nx, rows, width), scratch(rows, width),
            scratch(rows, width, kind=F32), scratch(rows, width, kind=F32),
            by_y, by_y, by_g, by_g, by_g, by_g, by_y, by_y,
            scratch(nx, width, width, kind=F32),
            scratch(2, ny, nx, band, width), scratch(2, ny - 1, nx, band, width),
            scratch(2, nz, band, piece, kind=F32), scratch(2, nz - 1, band, piece, kind=F32),
            scratch(2, band, piece),
        ]
        semaphores = [
            pltpu.SemaphoreType.DMA((9,)),
            sems(ng - 1), sems(ny - 1), sems(ny - 1), sems(ng - 1),
            sems(nx - 1), sems(nx - 1), sems(1), sems(nx - 1), sems(1),
            sems(nx - 1), sems(1), sems(ny - 1), sems(ng - 1), sems(ng - 1), sems(ny - 1),
            sems(ny - 1, 2), sems(ny - 1, 2), sems(nz, 2), sems(ny - 1, 2), sems(ny, 2),
        ]
        shapes = (
            jax.ShapeDtypeStruct((rows, width), BF16),
            jax.ShapeDtypeStruct((rows, width), BF16),
            jax.ShapeDtypeStruct((2, width, full), BF16),
        )
        results = pl.pallas_call(
            functools.partial(kernel, (ny, nz, nx)),
            out_shape=tuple(pltpu.VMEM(v.shape, v.dtype) for v in shapes),
            in_specs=[pl.BlockSpec(memory_space=pltpu.HBM)] * 9,
            out_specs=(vmem, vmem, vmem),
            scratch_shapes=buffers + semaphores,
            compiler_params=pltpu.CompilerParams(
                collective_id=0, has_side_effects=True, vmem_limit_bytes=32 * 2**20
            ),
        )(
            *(
                pltpu.with_memory_space_constraint(v, pltpu.HBM)
                for v in (
                    features, w_self, w_neigh, grad_out, mirror_list.T, mirror_count[None, :],
                    tile_dst[None, :], tile_src[None, :], tiles,
                )
            )
        )
        weight = jax.ShapeDtypeStruct((width, full), BF16)
        return pl.pallas_call(
            write_out,
            out_shape=shapes[:2] + (weight, weight),
            in_specs=[vmem] * 3,
            out_specs=(stay,) * 4,
            scratch_shapes=[pltpu.SemaphoreType.DMA((4,))],
        )(*(pltpu.with_memory_space_constraint(v, pltpu.VMEM) for v in results))

    in_specs = (
        P("dom", "rep"),
        P("rep", None),
        P("rep", None),
        P("dom", "rep"),
        P("dom", None),
        P("dom"),
        P("dom"),
        P("dom"),
        P("dom", None, None),
    )
    out_specs = (P("dom", "rep"), P("dom", "rep"), P("rep", None), P("rep", None))
    return jax.shard_map(local, mesh=mesh, in_specs=in_specs, out_specs=out_specs, check_vma=False)
```

```python
import functools

import jax
import jax.numpy as jnp
from jax import lax
from jax.experimental import pallas as pl
from jax.experimental.pallas import tpu as pltpu
from jax.sharding import PartitionSpec as P

MESH = pl.DeviceIdType.MESH
F32 = jnp.float32
BF16 = jnp.bfloat16
CORES = 2
GRIDS = {128: (8, 8), 8: (2, 2)}

NN = (((1,), (0,)), ((), ()))
TN = (((0,), (0,)), ((), ()))
NT = (((1,), (1,)), ((), ()))


def dot(a, b, dims=NN):
    return lax.dot_general(a, b, dims, preferred_element_type=F32)


class Exchange:
    def __init__(self, n, me, device, src, dst, send_sem, recv_sem):
        self.n, self.me, self.device = n, me, device
        self.src, self.dst = src, dst
        self.send_sem, self.recv_sem = send_sem, recv_sem

    def copy(self, k, src, dst, peer):
        return pltpu.make_async_remote_copy(
            src_ref=src,
            dst_ref=dst,
            send_sem=self.send_sem.at[k - 1],
            recv_sem=self.recv_sem.at[k - 1],
            device_id=self.device(peer),
            device_id_type=MESH,
        )

    def each(self, step):
        if self.n == 2:
            step(1)
        else:
            lax.fori_loop(1, self.n, lambda k, c: (step(k), c)[1], 0)

    def outgoing(self, k):
        peer = lax.rem(self.me + k, self.n)
        return self.copy(k, self.src(peer), self.dst(self.me, k), peer)

    def start(self):
        if self.n == 2:
            self.outgoing(1).start()
            return

        def step(j, carry):
            k = self.n // 2 + lax.div(j + 1, 2) * (1 - 2 * lax.rem(j, 2))
            self.outgoing(k).start()
            return carry

        lax.fori_loop(0, self.n - 1, step, 0)

    def wait_send(self):
        self.each(lambda k: self.outgoing(k).wait_send())

    def wait_recv_one(self, k):
        peer = lax.rem(self.me - k + self.n, self.n)
        slot = self.dst(peer, k)
        self.copy(k, slot, slot, peer).wait_recv()

    def wait_recv(self):
        self.each(self.wait_recv_one)


def kernel(
    dims,
    feat_in, w_self_in, w_neigh_in, grad_out_in, list_in, count_in, dst_in, src_in, tiles_in,
    hidden, grad_feat, out_w,
    weights, grad_out, list_t, count, tile_dst, tile_src, tiles,
    perm01, perm10, hot0, hot1, edges, degree, table,
    o0, a0, s0, b0, o1, a1, s1, b1,
    acts, acts_peer, w_cols, pre_act, grads, grads_peer, direct, grad_agg,
    c0, d0, e0, f0, c1, d1, e1, f1,
    w_acc, wa_send, wa_recv, wb_send, wb_recv, wt_send,
    in_sem,
    sem_a0, sem_a1, sem_b0, sem_b1, sem_feat, sem_cols, sem_cols_core, sem_agg, sem_acts,
    sem_gather, sem_pass, sem_d0, sem_d1, sem_f0, sem_f1, sem_first, sem_second,
    sem_third, sem_fourth, sem_swap,
):
    ny, nz, nx = dims
    ng = nz * CORES
    nd = ny * ng
    rows, width = feat_in.shape
    half = width // 2
    slots = list_in.shape[0]
    entries = nd * slots
    tile_count, tile_rows = tiles_in.shape[0], tiles_in.shape[1]
    dst_count = rows // tile_rows
    src_count = (rows + entries) // tile_rows
    parts = nz // nx
    band, piece = half // ny, width // parts

    dom = lax.axis_index("dom")
    x = lax.axis_index("rep")
    y = lax.div(dom, ng)
    g = lax.rem(dom, ng)
    z = lax.div(g, CORES)
    c = lax.rem(g, CORES)

    def at_g(peer):
        return (y * ng + peer, x)

    def at_y(peer):
        return (peer * ng + g, x)

    def at_z(peer):
        return (y * ng + peer * CORES + c, x)

    def at_c(peer):
        return (y * ng + z * CORES + peer, x)

    def at_x(peer):
        return (dom, peer)

    def fetch(i, src, dst):
        return pltpu.make_async_copy(src, dst, in_sem.at[i])

    fetches = [
        fetch(0, list_in, list_t),
        fetch(1, count_in, count),
        fetch(2, feat_in, acts.at[0, x]),
        fetch(3, w_self_in, weights.at[0]),
        fetch(4, w_neigh_in, weights.at[1]),
        fetch(5, dst_in, tile_dst),
        fetch(6, src_in, tile_src),
        fetch(7, tiles_in, tiles),
        fetch(8, grad_out_in, grad_out),
    ]
    barrier = pltpu.get_barrier_semaphore()

    def greet_one(device):
        pl.semaphore_signal(barrier, inc=1, device_id=device, device_id_type=MESH)

    def greet(n, me, device):
        def step(k, carry):
            greet_one(device(lax.rem(me + k, n)))
            return carry

        lax.fori_loop(1, n, step, 0)

    greet(ng, g, at_g)
    greet(ny, y, at_y)
    greet(nx, x, at_x)

    ways = (dict(n=ny, me=y, at=at_y), dict(n=nz, me=z, at=at_z))

    def across(h, i, column):
        return (ways[1 - h]["at"](i)[0], column)

    def senders(h, step):
        def one(k, carry):
            i, column = x * parts + lax.div(k, nx), lax.rem(k, nx)

            @pl.when(jnp.logical_or(i != ways[1 - h]["me"], column != x))
            def _():
                step(k, i, column)

            return carry

        lax.fori_loop(0, parts * nx, one, 0)

    expected = (ng - 1) + (ny - 1) + (nx - 1)
    for h in range(2):
        senders(h, lambda k, i, column: greet_one(across(h, i, column)))
        after = ways[1 - h]
        mine = (lax.div(after["me"], parts) == x).astype(jnp.int32)
        expected = expected + after["n"] - mine

    for f in fetches:
        f.start()

    def iota(shape, axis):
        return lax.broadcasted_iota(jnp.int32, shape, axis)

    col = iota((1, entries), 1)
    row = iota((entries, entries), 0)

    def selection(index):
        return jnp.where(row == index, 1.0, 0.0).astype(BF16)

    from_listed = selection(lax.rem(col, slots) * nd + lax.div(col, slots))
    y_in = lax.rem(lax.div(col, slots), ny)
    g_in = lax.div(col, slots * ny)
    slot_in = lax.rem(col, slots)
    perm01[...] = selection((y_in * ng + g_in) * slots + slot_in)

    fetches[0].wait()
    fetches[1].wait()
    listed = jnp.concatenate(
        [jnp.where(j < count[...], list_t[j : j + 1, :], -1) for j in range(slots)], axis=1
    )
    listed = jnp.broadcast_to(listed.astype(F32), (8, entries)).astype(BF16)
    natural = dot(listed, from_listed)
    transposed = dot(natural.astype(BF16), perm01[...])
    vertex = iota((rows, entries), 0).astype(F32)
    hot0[...] = jnp.where(vertex == transposed[0:1, :], 1.0, 0.0).astype(BF16)
    hot1[...] = jnp.where(vertex == natural[0:1, :], 1.0, 0.0).astype(BF16)
    per_g, per_y = entries // ng, entries // ny
    fetches[2].wait()
    feat = acts[0, x]
    o0[...] = dot(hot0[...], feat[:, :half], TN).astype(BF16).reshape(ng, per_g, half)
    o1[...] = dot(hot1[...], feat[:, half:], TN).astype(BF16).reshape(ny, per_y, half)

    pl.semaphore_wait(barrier, expected)

    out_a0 = Exchange(ng, g, at_g, lambda p: o0.at[p], lambda s, k: a0.at[s], *sem_pair(sem_a0))
    out_a1 = Exchange(ny, y, at_y, lambda p: o1.at[p], lambda s, k: a1.at[s], *sem_pair(sem_a1))
    out_b0 = Exchange(ny, y, at_y, lambda p: s0.at[p], lambda s, k: b0.at[s], *sem_pair(sem_b0))
    out_b1 = Exchange(ng, g, at_g, lambda p: s1.at[p], lambda s, k: b1.at[s], *sem_pair(sem_b1))
    out_a0.start()
    out_a1.start()

    def columns(p):
        return pl.ds(pl.multiple_of(p * width, width), width)

    feats = Exchange(
        nx, x, at_x, lambda p: acts.at[0, x], lambda s, k: acts.at[0, s], *sem_pair(sem_feat)
    )
    cols = Exchange(
        nx, x, at_x, lambda p: weights.at[c, :, columns(p)], lambda s, k: w_cols.at[c, s],
        *sem_pair(sem_cols)
    )
    cols_core = Exchange(
        CORES, c, at_c, lambda p: w_cols.at[c], lambda s, k: w_cols.at[s], *sem_pair(sem_cols_core)
    )
    fetches[3].wait()
    fetches[4].wait()
    cols.start()
    feats.start()
    a0[g] = o0[g]
    a1[y] = o1[y]
    w_cols[c, x] = weights[c, :, columns(x)]
    table[:rows, :] = feat

    y_out = lax.div(col, slots * ng)
    g_out = lax.rem(lax.div(col, slots), ng)
    perm10[...] = selection((g_out * ny + y_out) * slots + slot_in)
    for f in fetches[5:]:
        f.wait()

    out_a0.wait_recv()
    s0[...] = dot(perm01[...], a0[...].reshape(entries, half)).astype(BF16).reshape(ny, per_y, half)
    out_b0.start()
    out_a1.wait_recv()
    s1[...] = dot(perm10[...], a1[...].reshape(entries, half)).astype(BF16).reshape(ng, per_g, half)
    out_b1.start()
    b0[y] = s0[y]
    b1[g] = s1[g]

    block_of = tile_dst[...] * src_count + tile_src[...]
    for i in range(dst_count):
        for j in range(src_count):
            here = jnp.where(block_of == i * src_count + j, 1.0, 0.0)
            total = jnp.zeros((tile_rows, tile_rows), F32)
            for t in range(tile_count):
                total += here[:, t : t + 1] * tiles[t].astype(F32)
            top = total.astype(BF16)
            at = (pl.ds(i * tile_rows, tile_rows), pl.ds(j * tile_rows, tile_rows))
            edges[(0,) + at] = top
            edges[(1,) + at] = (total - top.astype(F32)).astype(BF16)
    ones = jnp.ones((rows + entries, tile_rows), BF16)
    degree[...] = jnp.maximum(dot(edges[0], ones) + dot(edges[1], ones), 1.0)
    cols.wait_recv()
    cols_core.start()

    out_b0.wait_recv()
    table[rows:, :half] = b0[...].reshape(entries, half)
    out_b1.wait_recv()
    table[rows:, half:] = dot(perm01[...], b1[...].reshape(entries, half)).astype(BF16)

    safe = jnp.concatenate([degree[...]] * (width // tile_rows), axis=1)
    summed = dot(edges[0], table[...]) + dot(edges[1], table[...])
    acts[1, x] = (summed / safe).astype(BF16)
    aggs = Exchange(
        nx, x, at_x, lambda p: acts.at[1, x], lambda s, k: acts.at[1, s], *sem_pair(sem_agg)
    )
    aggs.start()

    def pass_acts(k):
        q = lax.rem(x - k + nx, nx)
        return Exchange(
            CORES, c, at_c, lambda p: acts.at[p, q], lambda s, i: acts_peer.at[q],
            *(sem.at[pl.ds(k, 1)] for sem in sem_pair(sem_acts))
        )

    feats.wait_recv()
    send_acts = [pass_acts(k) for k in range(nx)]
    send_acts[0].start()
    cols_core.wait_recv()
    total = dot(acts[1, x], w_cols[1, x])
    for q in range(nx):
        total += dot(acts[0, q], w_cols[0, q])
    pre_act[...] = total
    for k in range(1, nx):
        q = lax.rem(x - k + nx, nx)
        aggs.wait_recv_one(k)
        send_acts[k].start()
        pre_act[...] += dot(acts[1, q], w_cols[1, q])
    value = pre_act[...]
    sig = jax.nn.sigmoid(value)
    grads[x] = (grad_out[...].astype(F32) * (sig + value * sig * (1.0 - sig))).astype(BF16)

    send_grads = Exchange(
        CORES, c, at_c, lambda p: grads.at[x], lambda s, k: grads_peer, *sem_pair(sem_pass)
    )
    gather = Exchange(
        nx, x, at_x, lambda p: grads.at[x], lambda s, k: grads.at[s], *sem_pair(sem_gather)
    )
    send_grads.start()
    gather.start()
    hidden[...] = (value * sig).astype(BF16)

    for q in range(nx):
        w_acc[q] = dot(acts[c, q], grads[x], TN)
    for done in send_acts:
        done.wait_recv()
    send_grads.wait_recv()
    for q in range(nx):
        block = w_acc[q] + dot(acts_peer[q], grads_peer[...], TN)
        w_acc[q] = block
        block = block.astype(BF16)
        for h in range(2):
            wa_send[h, :, q] = block[h * half : (h + 1) * half, :].reshape(ny, band, width)

    def first(h):
        way = ways[h]
        return Exchange(
            way["n"], way["me"], way["at"], lambda p: wa_send.at[h, p],
            lambda s, k: wa_recv.at[h, k - 1], *sem_pair(sem_first, h)
        )

    firsts = [first(0), first(1)]
    for way in firsts:
        way.start()

    direct[...] = dot(grads[x], weights[0, :, columns(x)], NT)
    grad_agg[...] = dot(grads[x], weights[1, :, columns(x)], NT)
    for k in range(1, nx):
        q = lax.rem(x - k + nx, nx)
        gather.wait_recv_one(k)
        direct[...] += dot(grads[q], weights[0, :, columns(q)], NT)
        grad_agg[...] += dot(grads[q], weights[1, :, columns(q)], NT)
    scaled = (grad_agg[...] / safe).astype(BF16)
    table_grad = dot(edges[0], scaled, TN) + dot(edges[1], scaled, TN)
    direct[...] += table_grad[:rows, :]
    mirror = table_grad[rows:, :].astype(BF16)

    c0[...] = mirror[:, :half].reshape(ny, per_y, half)
    c1[...] = dot(perm10[...], mirror[:, half:]).astype(BF16).reshape(ng, per_g, half)
    back_d0 = Exchange(ny, y, at_y, lambda p: c0.at[p], lambda s, k: d0.at[s], *sem_pair(sem_d0))
    back_d1 = Exchange(ng, g, at_g, lambda p: c1.at[p], lambda s, k: d1.at[s], *sem_pair(sem_d1))
    back_f0 = Exchange(ng, g, at_g, lambda p: e0.at[p], lambda s, k: f0.at[s], *sem_pair(sem_f0))
    back_f1 = Exchange(ny, y, at_y, lambda p: e1.at[p], lambda s, k: f1.at[s], *sem_pair(sem_f1))
    back_d0.start()
    back_d1.start()
    d0[y] = c0[y]
    d1[g] = c1[g]

    def second(h):
        way = ways[1 - h]
        return Exchange(
            way["n"], way["me"], way["at"], lambda p: wb_send.at[h, p],
            lambda s, k: wb_recv.at[h, k - 1], *sem_pair(sem_second, h)
        )

    seconds = [second(0), second(1)]
    for h in range(2):
        firsts[h].wait_recv()
        way, after = ways[h], ways[1 - h]
        own_rows = pl.ds(pl.multiple_of(h * half + way["me"] * band, band), band)
        for q in range(nx):
            total = w_acc[q, own_rows, :]
            for k in range(way["n"] - 1):
                total = total + wa_recv[h, k, q].astype(F32)
            for i in range(parts):
                wb_send[h, q * parts + i] = total[:, i * piece : (i + 1) * piece]
        seconds[h].start()

    scale = float(rows * nd) ** (-0.5)

    def piece_at(h, i, column):
        r = h * half + ways[h]["me"] * band
        q = column * width + lax.rem(i, parts) * piece
        return out_w.at[c, pl.ds(pl.multiple_of(r, band), band), pl.ds(pl.multiple_of(q, piece), piece)]

    def third(h, k, dst, device, slot):
        return pltpu.make_async_remote_copy(
            src_ref=wt_send.at[h], dst_ref=dst, send_sem=sem_third.at[h, 0, k],
            recv_sem=sem_third.at[h, 1, slot], device_id=device, device_id_type=MESH,
        )

    def thirds(h, step):
        after = ways[1 - h]
        me = after["me"]
        slot = lax.rem(me, parts) * nx + x
        target = lax.div(me, parts)

        def one(k, carry):
            copy = third(h, k, piece_at(h, me, x), across(h, lax.rem(me + k, after["n"]), target), slot)

            @pl.when(jnp.logical_or(k != 0, target != x))
            def _():
                step(copy)

            return carry

        lax.fori_loop(0, after["n"], one, 0)

    for h in range(2):
        seconds[h].wait_recv()
        after = ways[1 - h]
        total = wb_send[h, after["me"]]
        for k in range(after["n"] - 1):
            total = total + wb_recv[h, k]
        wt_send[h] = (total * scale).astype(BF16)
        thirds(h, lambda copy: copy.start())

        @pl.when(lax.div(after["me"], parts) == x)
        def _():
            piece_at(h, after["me"], x)[...] = wt_send[h]

    back_d0.wait_recv()
    e0[...] = dot(perm10[...], d0[...].reshape(entries, half)).astype(BF16).reshape(ng, per_g, half)
    back_f0.start()
    back_d1.wait_recv()
    e1[...] = dot(perm01[...], d1[...].reshape(entries, half)).astype(BF16).reshape(ny, per_y, half)
    back_f1.start()
    f0[g] = e0[g]
    f1[y] = e1[y]

    def band_at(h, i, core):
        return out_w.at[core, pl.ds(pl.multiple_of(h * half + i * band, band), band), :]

    def fourth(h):
        way = ways[h]
        return Exchange(
            way["n"], way["me"], way["at"], lambda p: band_at(h, way["me"], c),
            lambda s, k: band_at(h, s, c), *sem_pair(sem_fourth, h)
        )

    def swap(h, k):
        way = ways[h]
        i = lax.rem(way["me"] - k + way["n"], way["n"])
        return pltpu.make_async_remote_copy(
            src_ref=band_at(h, i, c), dst_ref=band_at(h, i, c), send_sem=sem_swap.at[h, 0, k],
            recv_sem=sem_swap.at[h, 1, k], device_id=at_c(1 - c), device_id_type=MESH,
        )

    fourths = [fourth(0), fourth(1)]
    for h in range(2):
        senders(
            h,
            lambda k, i, column: third(h, 0, piece_at(h, i, column), across(h, i, column), k).wait_recv(),
        )
        fourths[h].start()
        swap(h, 0).start()

    back_f0.wait_recv()
    grad_feat[:, :half] = (
        direct[:, :half] + dot(hot0[...], f0[...].reshape(entries, half))
    ).astype(BF16)
    back_f1.wait_recv()
    grad_feat[:, half:] = (
        direct[:, half:] + dot(hot1[...], f1[...].reshape(entries, half))
    ).astype(BF16)

    def pass_on(k):
        for h in range(2):
            fourths[h].wait_recv_one(k)
            swap(h, k).start()

    fourths[0].each(pass_on)

    def swapped(k, carry):
        for h in range(2):
            swap(h, k).wait_recv()
            swap(h, k).wait_send()
        return carry

    lax.fori_loop(0, ny, swapped, 0)
    for h in range(2):
        thirds(h, lambda copy: copy.wait_send())
    for done in (
        [out_a0, out_a1, out_b0, out_b1, feats, cols, cols_core, aggs, send_grads]
        + [gather, back_d0, back_d1, back_f0, back_f1] + send_acts + firsts + seconds + fourths
    ):
        done.wait_send()


def write_out(hidden, grad_feat, both, out0, out1, out2, out3, sem):
    pairs = ((hidden, out0), (grad_feat, out1), (both.at[0], out2), (both.at[1], out3))
    copies = [pltpu.make_async_copy(src, dst, sem.at[i]) for i, (src, dst) in enumerate(pairs)]
    for copy in copies:
        copy.start()
    for copy in copies:
        copy.wait()


def sem_pair(sems, use=0):
    return sems.at[use, 0], sems.at[use, 1]


def solution(mesh):
    doms, nx = mesh.shape["dom"], mesh.shape["rep"]
    ny, nz = GRIDS[doms]
    ng = nz * CORES

    def local(
        features, w_self, w_neigh, grad_out, mirror_list, mirror_count, tile_dst, tile_src, tiles
    ):
        rows, width = features.shape
        half, full = width // 2, width * nx
        slots = mirror_list.shape[1]
        entries = doms * slots
        tile_count, tile_rows = tiles.shape[0], tiles.shape[1]
        per_g, per_y = entries // ng, entries // ny
        assert ny == nz and rows == width and nz % nx == 0
        parts = nz // nx
        band, piece = half // ny, width // parts
        vmem, stay = (pl.BlockSpec(memory_space=s) for s in (pltpu.VMEM, pl.ANY))

        def scratch(*shape, kind=BF16):
            return pltpu.VMEM(shape, kind)

        def sems(n, uses=1):
            return pltpu.SemaphoreType.DMA((uses, 2, n))

        by_g, by_y = scratch(ng, per_g, half), scratch(ny, per_y, half)
        buffers = [
            scratch(2, width, full), scratch(rows, width),
            scratch(slots, doms, kind=jnp.int32), scratch(1, doms, kind=jnp.int32),
            scratch(1, tile_count, kind=jnp.int32), scratch(1, tile_count, kind=jnp.int32),
            scratch(tile_count, tile_rows, tile_rows),
            scratch(entries, entries), scratch(entries, entries),
            scratch(rows, entries), scratch(rows, entries),
            scratch(2, rows, rows + entries), scratch(rows, tile_rows, kind=F32),
            scratch(rows + entries, width),
            by_g, by_g, by_y, by_y, by_y, by_y, by_g, by_g,
            scratch(2, nx, rows, width), scratch(nx, rows, width), scratch(2, nx, width, width),
            scratch(rows, width, kind=F32), scratch(nx, rows, width), scratch(rows, width),
            scratch(rows, width, kind=F32), scratch(rows, width, kind=F32),
            by_y, by_y, by_g, by_g, by_g, by_g, by_y, by_y,
            scratch(nx, width, width, kind=F32),
            scratch(2, ny, nx, band, width), scratch(2, ny - 1, nx, band, width),
            scratch(2, nz, band, piece, kind=F32), scratch(2, nz - 1, band, piece, kind=F32),
            scratch(2, band, piece),
        ]
        semaphores = [
            pltpu.SemaphoreType.DMA((9,)),
            sems(ng - 1), sems(ny - 1), sems(ny - 1), sems(ng - 1),
            sems(nx - 1), sems(nx - 1), sems(1), sems(nx - 1), sems(nx),
            sems(nx - 1), sems(1), sems(ny - 1), sems(ng - 1), sems(ng - 1), sems(ny - 1),
            sems(ny - 1, 2), sems(ny - 1, 2), sems(nz, 2), sems(ny - 1, 2), sems(ny, 2),
        ]
        shapes = (
            jax.ShapeDtypeStruct((rows, width), BF16),
            jax.ShapeDtypeStruct((rows, width), BF16),
            jax.ShapeDtypeStruct((2, width, full), BF16),
        )
        results = pl.pallas_call(
            functools.partial(kernel, (ny, nz, nx)),
            out_shape=tuple(pltpu.VMEM(v.shape, v.dtype) for v in shapes),
            in_specs=[pl.BlockSpec(memory_space=pltpu.HBM)] * 9,
            out_specs=(vmem, vmem, vmem),
            scratch_shapes=buffers + semaphores,
            compiler_params=pltpu.CompilerParams(
                collective_id=0, has_side_effects=True, vmem_limit_bytes=32 * 2**20
            ),
        )(
            *(
                pltpu.with_memory_space_constraint(v, pltpu.HBM)
                for v in (
                    features, w_self, w_neigh, grad_out, mirror_list.T, mirror_count[None, :],
                    tile_dst[None, :], tile_src[None, :], tiles,
                )
            )
        )
        weight = jax.ShapeDtypeStruct((width, full), BF16)
        return pl.pallas_call(
            write_out,
            out_shape=shapes[:2] + (weight, weight),
            in_specs=[vmem] * 3,
            out_specs=(stay,) * 4,
            scratch_shapes=[pltpu.SemaphoreType.DMA((4,))],
        )(*(pltpu.with_memory_space_constraint(v, pltpu.VMEM) for v in results))

    in_specs = (
        P("dom", "rep"),
        P("rep", None),
        P("rep", None),
        P("dom", "rep"),
        P("dom", None),
        P("dom"),
        P("dom"),
        P("dom"),
        P("dom", None, None),
    )
    out_specs = (P("dom", "rep"), P("dom", "rep"), P("rep", None), P("rep", None))
    return jax.shard_map(local, mesh=mesh, in_specs=in_specs, out_specs=out_specs, check_vma=False)
```

```python
import functools

import jax
import jax.numpy as jnp
from jax import lax
from jax.experimental import pallas as pl
from jax.experimental.pallas import tpu as pltpu
from jax.sharding import PartitionSpec as P

MESH = pl.DeviceIdType.MESH
F32 = jnp.float32
BF16 = jnp.bfloat16
CORES = 2
GRIDS = {128: (8, 8), 8: (2, 2)}

NN = (((1,), (0,)), ((), ()))
TN = (((0,), (0,)), ((), ()))
NT = (((1,), (1,)), ((), ()))


def dot(a, b, dims=NN):
    return lax.dot_general(a, b, dims, preferred_element_type=F32)


class Exchange:
    def __init__(self, n, me, device, src, dst, send_sem, recv_sem):
        self.n, self.me, self.device = n, me, device
        self.src, self.dst = src, dst
        self.send_sem, self.recv_sem = send_sem, recv_sem

    def copy(self, k, src, dst, peer):
        return pltpu.make_async_remote_copy(
            src_ref=src,
            dst_ref=dst,
            send_sem=self.send_sem.at[k - 1],
            recv_sem=self.recv_sem.at[k - 1],
            device_id=self.device(peer),
            device_id_type=MESH,
        )

    def each(self, step):
        if self.n == 2:
            step(1)
        else:
            lax.fori_loop(1, self.n, lambda k, c: (step(k), c)[1], 0)

    def outgoing(self, k):
        peer = lax.rem(self.me + k, self.n)
        return self.copy(k, self.src(peer), self.dst(self.me, k), peer)

    def start(self):
        if self.n == 2:
            self.outgoing(1).start()
            return

        def step(j, carry):
            k = self.n // 2 + lax.div(j + 1, 2) * (1 - 2 * lax.rem(j, 2))
            self.outgoing(k).start()
            return carry

        lax.fori_loop(0, self.n - 1, step, 0)

    def wait_send(self):
        self.each(lambda k: self.outgoing(k).wait_send())

    def wait_recv_one(self, k):
        peer = lax.rem(self.me - k + self.n, self.n)
        slot = self.dst(peer, k)
        self.copy(k, slot, slot, peer).wait_recv()

    def wait_recv(self):
        self.each(self.wait_recv_one)


def kernel(
    dims,
    feat_in, w_self_in, w_neigh_in, grad_out_in, list_in, count_in, dst_in, src_in, tiles_in,
    hidden, grad_feat, out_w,
    weights, grad_out, list_t, count, tile_dst, tile_src, tiles,
    perm01, perm10, hot0, hot1, edges, degree, table,
    o0, a0, s0, b0, o1, a1, s1, b1,
    acts, acts_peer, w_cols, pre_act, grads, grads_peer, direct, grad_agg,
    c0, d0, e0, f0, c1, d1, e1, f1,
    w_acc, wa_send, wa_recv, wb_send, wb_recv,
    in_sem,
    sem_a0, sem_a1, sem_b0, sem_b1, sem_feat, sem_cols, sem_cols_core, sem_agg, sem_acts,
    sem_gather, sem_pass, sem_d0, sem_d1, sem_f0, sem_f1, sem_first, sem_second,
    sem_fourth, sem_swap,
):
    ny, nz, nx = dims
    ng = nz * CORES
    nd = ny * ng
    rows, width = feat_in.shape
    half = width // 2
    slots = list_in.shape[0]
    entries = nd * slots
    tile_count, tile_rows = tiles_in.shape[0], tiles_in.shape[1]
    dst_count = rows // tile_rows
    src_count = (rows + entries) // tile_rows
    band = half // ny

    dom = lax.axis_index("dom")
    x = lax.axis_index("rep")
    y = lax.div(dom, ng)
    g = lax.rem(dom, ng)
    z = lax.div(g, CORES)
    c = lax.rem(g, CORES)

    def at_g(peer):
        return (y * ng + peer, x)

    def at_y(peer):
        return (peer * ng + g, x)

    def at_z(peer):
        return (y * ng + peer * CORES + c, x)

    def at_c(peer):
        return (y * ng + z * CORES + peer, x)

    def at_x(peer):
        return (dom, peer)

    def fetch(i, src, dst):
        return pltpu.make_async_copy(src, dst, in_sem.at[i])

    fetches = [
        fetch(0, list_in, list_t),
        fetch(1, count_in, count),
        fetch(2, feat_in, acts.at[0, x]),
        fetch(3, w_self_in, weights.at[0]),
        fetch(4, w_neigh_in, weights.at[1]),
        fetch(5, dst_in, tile_dst),
        fetch(6, src_in, tile_src),
        fetch(7, tiles_in, tiles),
        fetch(8, grad_out_in, grad_out),
    ]
    barrier = pltpu.get_barrier_semaphore()

    def greet_one(device):
        pl.semaphore_signal(barrier, inc=1, device_id=device, device_id_type=MESH)

    def greet(n, me, device):
        def step(k, carry):
            greet_one(device(lax.rem(me + k, n)))
            return carry

        lax.fori_loop(1, n, step, 0)

    greet(ng, g, at_g)
    greet(ny, y, at_y)
    greet(nx, x, at_x)
    expected = (ng - 1) + (ny - 1) + (nx - 1)

    ways = (dict(n=ny, me=y, at=at_y), dict(n=nz, me=z, at=at_z))

    for f in fetches:
        f.start()

    def iota(shape, axis):
        return lax.broadcasted_iota(jnp.int32, shape, axis)

    col = iota((1, entries), 1)
    row = iota((entries, entries), 0)

    def selection(index):
        return jnp.where(row == index, 1.0, 0.0).astype(BF16)

    from_listed = selection(lax.rem(col, slots) * nd + lax.div(col, slots))
    y_in = lax.rem(lax.div(col, slots), ny)
    g_in = lax.div(col, slots * ny)
    slot_in = lax.rem(col, slots)
    perm01[...] = selection((y_in * ng + g_in) * slots + slot_in)

    fetches[0].wait()
    fetches[1].wait()
    listed = jnp.concatenate(
        [jnp.where(j < count[...], list_t[j : j + 1, :], -1) for j in range(slots)], axis=1
    )
    listed = jnp.broadcast_to(listed.astype(F32), (8, entries)).astype(BF16)
    natural = dot(listed, from_listed)
    transposed = dot(natural.astype(BF16), perm01[...])
    vertex = iota((rows, entries), 0).astype(F32)
    hot0[...] = jnp.where(vertex == transposed[0:1, :], 1.0, 0.0).astype(BF16)
    hot1[...] = jnp.where(vertex == natural[0:1, :], 1.0, 0.0).astype(BF16)
    per_g, per_y = entries // ng, entries // ny
    fetches[2].wait()
    feat = acts[0, x]
    o0[...] = dot(hot0[...], feat[:, :half], TN).astype(BF16).reshape(ng, per_g, half)
    o1[...] = dot(hot1[...], feat[:, half:], TN).astype(BF16).reshape(ny, per_y, half)

    pl.semaphore_wait(barrier, expected)

    out_a0 = Exchange(ng, g, at_g, lambda p: o0.at[p], lambda s, k: a0.at[s], *sem_pair(sem_a0))
    out_a1 = Exchange(ny, y, at_y, lambda p: o1.at[p], lambda s, k: a1.at[s], *sem_pair(sem_a1))
    out_b0 = Exchange(ny, y, at_y, lambda p: s0.at[p], lambda s, k: b0.at[s], *sem_pair(sem_b0))
    out_b1 = Exchange(ng, g, at_g, lambda p: s1.at[p], lambda s, k: b1.at[s], *sem_pair(sem_b1))
    out_a0.start()
    out_a1.start()

    def columns(p):
        return pl.ds(pl.multiple_of(p * width, width), width)

    feats = Exchange(
        nx, x, at_x, lambda p: acts.at[0, x], lambda s, k: acts.at[0, s], *sem_pair(sem_feat)
    )
    cols = Exchange(
        nx, x, at_x, lambda p: weights.at[c, :, columns(p)], lambda s, k: w_cols.at[c, s],
        *sem_pair(sem_cols)
    )
    cols_core = Exchange(
        CORES, c, at_c, lambda p: w_cols.at[c], lambda s, k: w_cols.at[s], *sem_pair(sem_cols_core)
    )
    fetches[3].wait()
    fetches[4].wait()
    cols.start()
    feats.start()
    a0[g] = o0[g]
    a1[y] = o1[y]
    w_cols[c, x] = weights[c, :, columns(x)]
    table[:rows, :] = feat

    y_out = lax.div(col, slots * ng)
    g_out = lax.rem(lax.div(col, slots), ng)
    perm10[...] = selection((g_out * ny + y_out) * slots + slot_in)
    for f in fetches[5:]:
        f.wait()

    out_a0.wait_recv()
    s0[...] = dot(perm01[...], a0[...].reshape(entries, half)).astype(BF16).reshape(ny, per_y, half)
    out_b0.start()
    out_a1.wait_recv()
    s1[...] = dot(perm10[...], a1[...].reshape(entries, half)).astype(BF16).reshape(ng, per_g, half)
    out_b1.start()
    b0[y] = s0[y]
    b1[g] = s1[g]

    block_of = tile_dst[...] * src_count + tile_src[...]
    for i in range(dst_count):
        for j in range(src_count):
            here = jnp.where(block_of == i * src_count + j, 1.0, 0.0)
            total = jnp.zeros((tile_rows, tile_rows), F32)
            for t in range(tile_count):
                total += here[:, t : t + 1] * tiles[t].astype(F32)
            top = total.astype(BF16)
            at = (pl.ds(i * tile_rows, tile_rows), pl.ds(j * tile_rows, tile_rows))
            edges[(0,) + at] = top
            edges[(1,) + at] = (total - top.astype(F32)).astype(BF16)
    ones = jnp.ones((rows + entries, tile_rows), BF16)
    degree[...] = jnp.maximum(dot(edges[0], ones) + dot(edges[1], ones), 1.0)
    cols.wait_recv()
    cols_core.start()

    out_b0.wait_recv()
    table[rows:, :half] = b0[...].reshape(entries, half)
    out_b1.wait_recv()
    table[rows:, half:] = dot(perm01[...], b1[...].reshape(entries, half)).astype(BF16)

    safe = jnp.concatenate([degree[...]] * (width // tile_rows), axis=1)
    summed = dot(edges[0], table[...]) + dot(edges[1], table[...])
    acts[1, x] = (summed / safe).astype(BF16)
    aggs = Exchange(
        nx, x, at_x, lambda p: acts.at[1, x], lambda s, k: acts.at[1, s], *sem_pair(sem_agg)
    )
    aggs.start()

    def pass_acts(k):
        q = lax.rem(x - k + nx, nx)
        return Exchange(
            CORES, c, at_c, lambda p: acts.at[p, q], lambda s, i: acts_peer.at[q],
            *(sem.at[pl.ds(k, 1)] for sem in sem_pair(sem_acts))
        )

    feats.wait_recv()
    send_acts = [pass_acts(k) for k in range(nx)]
    send_acts[0].start()
    cols_core.wait_recv()
    total = dot(acts[1, x], w_cols[1, x])
    for q in range(nx):
        total += dot(acts[0, q], w_cols[0, q])
    pre_act[...] = total
    for k in range(1, nx):
        q = lax.rem(x - k + nx, nx)
        aggs.wait_recv_one(k)
        send_acts[k].start()
        pre_act[...] += dot(acts[1, q], w_cols[1, q])
    value = pre_act[...]
    sig = jax.nn.sigmoid(value)
    grads[x] = (grad_out[...].astype(F32) * (sig + value * sig * (1.0 - sig))).astype(BF16)

    send_grads = Exchange(
        CORES, c, at_c, lambda p: grads.at[x], lambda s, k: grads_peer, *sem_pair(sem_pass)
    )
    gather = Exchange(
        nx, x, at_x, lambda p: grads.at[x], lambda s, k: grads.at[s], *sem_pair(sem_gather)
    )
    send_grads.start()
    gather.start()
    hidden[...] = (value * sig).astype(BF16)

    for q in range(nx):
        w_acc[q] = dot(acts[c, q], grads[x], TN)
    for done in send_acts:
        done.wait_recv()
    send_grads.wait_recv()
    for q in range(nx):
        block = w_acc[q] + dot(acts_peer[q], grads_peer[...], TN)
        w_acc[q] = block
        block = block.astype(BF16)
        for h in range(2):
            wa_send[h, :, q] = block[h * half : (h + 1) * half, :].reshape(ny, band, width)

    def first(h):
        way = ways[h]
        return Exchange(
            way["n"], way["me"], way["at"], lambda p: wa_send.at[h, p],
            lambda s, k: wa_recv.at[h, k - 1], *sem_pair(sem_first, h)
        )

    firsts = [first(0), first(1)]
    for way in firsts:
        way.start()

    direct[...] = dot(grads[x], weights[0, :, columns(x)], NT)
    grad_agg[...] = dot(grads[x], weights[1, :, columns(x)], NT)
    for k in range(1, nx):
        q = lax.rem(x - k + nx, nx)
        gather.wait_recv_one(k)
        direct[...] += dot(grads[q], weights[0, :, columns(q)], NT)
        grad_agg[...] += dot(grads[q], weights[1, :, columns(q)], NT)
    scaled = (grad_agg[...] / safe).astype(BF16)
    table_grad = dot(edges[0], scaled, TN) + dot(edges[1], scaled, TN)
    direct[...] += table_grad[:rows, :]
    mirror = table_grad[rows:, :].astype(BF16)

    c0[...] = mirror[:, :half].reshape(ny, per_y, half)
    c1[...] = dot(perm10[...], mirror[:, half:]).astype(BF16).reshape(ng, per_g, half)
    back_d0 = Exchange(ny, y, at_y, lambda p: c0.at[p], lambda s, k: d0.at[s], *sem_pair(sem_d0))
    back_d1 = Exchange(ng, g, at_g, lambda p: c1.at[p], lambda s, k: d1.at[s], *sem_pair(sem_d1))
    back_f0 = Exchange(ng, g, at_g, lambda p: e0.at[p], lambda s, k: f0.at[s], *sem_pair(sem_f0))
    back_f1 = Exchange(ny, y, at_y, lambda p: e1.at[p], lambda s, k: f1.at[s], *sem_pair(sem_f1))
    back_d0.start()
    back_d1.start()
    d0[y] = c0[y]
    d1[g] = c1[g]

    def second(h):
        way = ways[1 - h]
        return Exchange(
            way["n"] * nx, way["me"] * nx + x,
            lambda p: (way["at"](lax.div(p, nx))[0], lax.rem(p, nx)),
            lambda p: wb_send.at[h, lax.rem(p, nx)], lambda s, k: wb_recv.at[h, s],
            *sem_pair(sem_second, h)
        )

    seconds = [second(0), second(1)]
    for h in range(2):
        firsts[h].wait_recv()
        way, after = ways[h], ways[1 - h]
        own_rows = pl.ds(pl.multiple_of(h * half + way["me"] * band, band), band)
        for q in range(nx):
            total = w_acc[q, own_rows, :]
            for k in range(way["n"] - 1):
                total = total + wa_recv[h, k, q].astype(F32)
            wb_send[h, q] = total.astype(BF16)
        seconds[h].start()
        wb_recv[h, after["me"] * nx + x] = wb_send[h, x]

    back_d0.wait_recv()
    e0[...] = dot(perm10[...], d0[...].reshape(entries, half)).astype(BF16).reshape(ng, per_g, half)
    back_f0.start()
    back_d1.wait_recv()
    e1[...] = dot(perm01[...], d1[...].reshape(entries, half)).astype(BF16).reshape(ny, per_y, half)
    back_f1.start()
    f0[g] = e0[g]
    f1[y] = e1[y]

    def band_at(h, i, core):
        return out_w.at[core, pl.ds(pl.multiple_of(h * half + i * band, band), band), :]

    def fourth(h):
        way = ways[h]
        return Exchange(
            way["n"], way["me"], way["at"], lambda p: band_at(h, way["me"], c),
            lambda s, k: band_at(h, s, c), *sem_pair(sem_fourth, h)
        )

    def swap(h, k):
        way = ways[h]
        i = lax.rem(way["me"] - k + way["n"], way["n"])
        return pltpu.make_async_remote_copy(
            src_ref=band_at(h, i, c), dst_ref=band_at(h, i, c), send_sem=sem_swap.at[h, 0, k],
            recv_sem=sem_swap.at[h, 1, k], device_id=at_c(1 - c), device_id_type=MESH,
        )

    fourths = [fourth(0), fourth(1)]
    scale = float(rows * nd) ** (-0.5)
    for h in range(2):
        seconds[h].wait_recv()
        mine = band_at(h, ways[h]["me"], c)
        for q in range(nx):
            total = wb_recv[h, q].astype(F32)
            for i in range(1, ways[1 - h]["n"]):
                total = total + wb_recv[h, i * nx + q].astype(F32)
            mine[:, pl.ds(q * width, width)] = (total * scale).astype(BF16)
        fourths[h].start()
        swap(h, 0).start()

    back_f0.wait_recv()
    grad_feat[:, :half] = (
        direct[:, :half] + dot(hot0[...], f0[...].reshape(entries, half))
    ).astype(BF16)
    back_f1.wait_recv()
    grad_feat[:, half:] = (
        direct[:, half:] + dot(hot1[...], f1[...].reshape(entries, half))
    ).astype(BF16)

    def pass_on(k):
        for h in range(2):
            fourths[h].wait_recv_one(k)
            swap(h, k).start()

    fourths[0].each(pass_on)

    def swapped(k, carry):
        for h in range(2):
            swap(h, k).wait_recv()
            swap(h, k).wait_send()
        return carry

    lax.fori_loop(0, ny, swapped, 0)
    for done in (
        [out_a0, out_a1, out_b0, out_b1, feats, cols, cols_core, aggs, send_grads]
        + [gather, back_d0, back_d1, back_f0, back_f1] + send_acts + firsts + seconds + fourths
    ):
        done.wait_send()


def write_out(hidden, grad_feat, both, out0, out1, out2, out3, sem):
    pairs = ((hidden, out0), (grad_feat, out1), (both.at[0], out2), (both.at[1], out3))
    copies = [pltpu.make_async_copy(src, dst, sem.at[i]) for i, (src, dst) in enumerate(pairs)]
    for copy in copies:
        copy.start()
    for copy in copies:
        copy.wait()


def sem_pair(sems, use=0):
    return sems.at[use, 0], sems.at[use, 1]


def solution(mesh):
    doms, nx = mesh.shape["dom"], mesh.shape["rep"]
    ny, nz = GRIDS[doms]
    ng = nz * CORES

    def local(
        features, w_self, w_neigh, grad_out, mirror_list, mirror_count, tile_dst, tile_src, tiles
    ):
        rows, width = features.shape
        half, full = width // 2, width * nx
        slots = mirror_list.shape[1]
        entries = doms * slots
        tile_count, tile_rows = tiles.shape[0], tiles.shape[1]
        per_g, per_y = entries // ng, entries // ny
        assert ny == nz and rows == width
        band = half // ny
        vmem, stay = (pl.BlockSpec(memory_space=s) for s in (pltpu.VMEM, pl.ANY))

        def scratch(*shape, kind=BF16):
            return pltpu.VMEM(shape, kind)

        def sems(n, uses=1):
            return pltpu.SemaphoreType.DMA((uses, 2, n))

        by_g, by_y = scratch(ng, per_g, half), scratch(ny, per_y, half)
        buffers = [
            scratch(2, width, full), scratch(rows, width),
            scratch(slots, doms, kind=jnp.int32), scratch(1, doms, kind=jnp.int32),
            scratch(1, tile_count, kind=jnp.int32), scratch(1, tile_count, kind=jnp.int32),
            scratch(tile_count, tile_rows, tile_rows),
            scratch(entries, entries), scratch(entries, entries),
            scratch(rows, entries), scratch(rows, entries),
            scratch(2, rows, rows + entries), scratch(rows, tile_rows, kind=F32),
            scratch(rows + entries, width),
            by_g, by_g, by_y, by_y, by_y, by_y, by_g, by_g,
            scratch(2, nx, rows, width), scratch(nx, rows, width), scratch(2, nx, width, width),
            scratch(rows, width, kind=F32), scratch(nx, rows, width), scratch(rows, width),
            scratch(rows, width, kind=F32), scratch(rows, width, kind=F32),
            by_y, by_y, by_g, by_g, by_g, by_g, by_y, by_y,
            scratch(nx, width, width, kind=F32),
            scratch(2, ny, nx, band, width), scratch(2, ny - 1, nx, band, width),
            scratch(2, nx, band, width), scratch(2, nz * nx, band, width),
        ]
        semaphores = [
            pltpu.SemaphoreType.DMA((9,)),
            sems(ng - 1), sems(ny - 1), sems(ny - 1), sems(ng - 1),
            sems(nx - 1), sems(nx - 1), sems(1), sems(nx - 1), sems(nx),
            sems(nx - 1), sems(1), sems(ny - 1), sems(ng - 1), sems(ng - 1), sems(ny - 1),
            sems(ny - 1, 2), sems(nz * nx - 1, 2), sems(ny - 1, 2), sems(ny, 2),
        ]
        shapes = (
            jax.ShapeDtypeStruct((rows, width), BF16),
            jax.ShapeDtypeStruct((rows, width), BF16),
            jax.ShapeDtypeStruct((2, width, full), BF16),
        )
        results = pl.pallas_call(
            functools.partial(kernel, (ny, nz, nx)),
            out_shape=tuple(pltpu.VMEM(v.shape, v.dtype) for v in shapes),
            in_specs=[pl.BlockSpec(memory_space=pltpu.HBM)] * 9,
            out_specs=(vmem, vmem, vmem),
            scratch_shapes=buffers + semaphores,
            compiler_params=pltpu.CompilerParams(
                collective_id=0, has_side_effects=True, vmem_limit_bytes=32 * 2**20
            ),
        )(
            *(
                pltpu.with_memory_space_constraint(v, pltpu.HBM)
                for v in (
                    features, w_self, w_neigh, grad_out, mirror_list.T, mirror_count[None, :],
                    tile_dst[None, :], tile_src[None, :], tiles,
                )
            )
        )
        weight = jax.ShapeDtypeStruct((width, full), BF16)
        return pl.pallas_call(
            write_out,
            out_shape=shapes[:2] + (weight, weight),
            in_specs=[vmem] * 3,
            out_specs=(stay,) * 4,
            scratch_shapes=[pltpu.SemaphoreType.DMA((4,))],
        )(*(pltpu.with_memory_space_constraint(v, pltpu.VMEM) for v in results))

    in_specs = (
        P("dom", "rep"),
        P("rep", None),
        P("rep", None),
        P("dom", "rep"),
        P("dom", None),
        P("dom"),
        P("dom"),
        P("dom"),
        P("dom", None, None),
    )
    out_specs = (P("dom", "rep"), P("dom", "rep"), P("rep", None), P("rep", None))
    return jax.shard_map(local, mesh=mesh, in_specs=in_specs, out_specs=out_specs, check_vma=False)
```

```python
import functools

import jax
import jax.numpy as jnp
from jax import lax
from jax.experimental import pallas as pl
from jax.experimental.pallas import tpu as pltpu
from jax.sharding import PartitionSpec as P

MESH = pl.DeviceIdType.MESH
F32 = jnp.float32
BF16 = jnp.bfloat16
CORES = 2
GRIDS = {128: (8, 8), 8: (2, 2)}

NN = (((1,), (0,)), ((), ()))
TN = (((0,), (0,)), ((), ()))
NT = (((1,), (1,)), ((), ()))


def dot(a, b, dims=NN):
    return lax.dot_general(a, b, dims, preferred_element_type=F32)


def far_first(n, j):
    return n // 2 + lax.div(j + 1, 2) * (1 - 2 * lax.rem(j, 2))


class Exchange:
    def __init__(self, n, me, device, src, dst, send_sem, recv_sem):
        self.n, self.me, self.device = n, me, device
        self.src, self.dst = src, dst
        self.send_sem, self.recv_sem = send_sem, recv_sem

    def copy(self, k, src, dst, peer):
        return pltpu.make_async_remote_copy(
            src_ref=src,
            dst_ref=dst,
            send_sem=self.send_sem.at[k - 1],
            recv_sem=self.recv_sem.at[k - 1],
            device_id=self.device(peer),
            device_id_type=MESH,
        )

    def each(self, step):
        if self.n == 2:
            step(1)
        else:
            lax.fori_loop(1, self.n, lambda k, c: (step(k), c)[1], 0)

    def outgoing(self, k):
        peer = lax.rem(self.me + k, self.n)
        return self.copy(k, self.src(peer), self.dst(self.me, k), peer)

    def start(self):
        if self.n == 2:
            self.outgoing(1).start()
            return

        def step(j, carry):
            self.outgoing(far_first(self.n, j)).start()
            return carry

        lax.fori_loop(0, self.n - 1, step, 0)

    def wait_send(self):
        self.each(lambda k: self.outgoing(k).wait_send())

    def wait_recv_one(self, k):
        peer = lax.rem(self.me - k + self.n, self.n)
        slot = self.dst(peer, k)
        self.copy(k, slot, slot, peer).wait_recv()

    def wait_recv(self):
        self.each(self.wait_recv_one)


def kernel(
    dims,
    feat_in, w_self_in, w_neigh_in, grad_out_in, list_in, count_in, dst_in, src_in, tiles_in,
    hidden, grad_feat, out_w,
    weights, grad_out, list_t, count, tile_dst, tile_src, tiles,
    perm01, perm10, hot0, hot1, edges, edges_t, degree, own_sum,
    o0, a0, s0, b0, o1, a1, s1, b1,
    acts, acts_peer, w_cols, pre_act, grads, grads_peer, direct, grad_agg,
    c0, d0, e0, f0, c1, d1, e1, f1,
    w_acc, wa_send, wa_recv, wb_send, wb_recv, wt_send,
    in_sem,
    sem_a0, sem_a1, sem_b0, sem_b1, sem_feat, sem_cols, sem_cols_core, sem_agg, sem_acts,
    sem_gather, sem_pass, sem_d0, sem_d1, sem_f0, sem_f1, sem_first, sem_second,
    sem_third, sem_fourth, sem_swap,
):
    ny, nz, nx = dims
    ng = nz * CORES
    nd = ny * ng
    rows, width = feat_in.shape
    half = width // 2
    slots = list_in.shape[0]
    entries = nd * slots
    tile_count, tile_rows = tiles_in.shape[0], tiles_in.shape[1]
    dst_count = rows // tile_rows
    src_count = (rows + entries) // tile_rows
    parts = nz // nx
    band, piece = half // ny, width // parts

    dom = lax.axis_index("dom")
    x = lax.axis_index("rep")
    y = lax.div(dom, ng)
    g = lax.rem(dom, ng)
    z = lax.div(g, CORES)
    c = lax.rem(g, CORES)

    def at_g(peer):
        return (y * ng + peer, x)

    def at_y(peer):
        return (peer * ng + g, x)

    def at_z(peer):
        return (y * ng + peer * CORES + c, x)

    def at_c(peer):
        return (y * ng + z * CORES + peer, x)

    def at_x(peer):
        return (dom, peer)

    def fetch(i, src, dst):
        return pltpu.make_async_copy(src, dst, in_sem.at[i])

    fetches = [
        fetch(0, list_in, list_t),
        fetch(1, count_in, count),
        fetch(2, feat_in, acts.at[0, x]),
        fetch(3, w_self_in, weights.at[0]),
        fetch(4, w_neigh_in, weights.at[1]),
        fetch(5, dst_in, tile_dst),
        fetch(6, src_in, tile_src),
        fetch(7, tiles_in, tiles),
        fetch(8, grad_out_in, grad_out),
    ]
    barrier = pltpu.get_barrier_semaphore()

    def greet_one(device):
        pl.semaphore_signal(barrier, inc=1, device_id=device, device_id_type=MESH)

    def greet(n, me, device):
        def step(j, carry):
            greet_one(device(lax.rem(me + far_first(n, j), n)))
            return carry

        lax.fori_loop(0, n - 1, step, 0)

    greet(ny, y, at_y)
    greet(ng, g, at_g)
    greet(nx, x, at_x)

    ways = (dict(n=ny, me=y, at=at_y), dict(n=nz, me=z, at=at_z))

    def across(h, i, column):
        return (ways[1 - h]["at"](i)[0], column)

    def senders(h, step):
        def one(k, carry):
            i, column = x * parts + lax.div(k, nx), lax.rem(k, nx)

            @pl.when(jnp.logical_or(i != ways[1 - h]["me"], column != x))
            def _():
                step(k, i, column)

            return carry

        lax.fori_loop(0, parts * nx, one, 0)

    expected = (ng - 1) + (ny - 1) + (nx - 1)
    for f in fetches:
        f.start()

    def iota(shape, axis):
        return lax.broadcasted_iota(jnp.int32, shape, axis)

    col = iota((1, entries), 1)
    row = iota((entries, entries), 0)

    def selection(index):
        return jnp.where(row == index, 1.0, 0.0).astype(BF16)

    from_listed = selection(lax.rem(col, slots) * nd + lax.div(col, slots))
    y_in = lax.rem(lax.div(col, slots), ny)
    g_in = lax.div(col, slots * ny)
    slot_in = lax.rem(col, slots)
    perm01[...] = selection((y_in * ng + g_in) * slots + slot_in)

    fetches[0].wait()
    fetches[1].wait()
    listed = jnp.concatenate(
        [jnp.where(j < count[...], list_t[j : j + 1, :], -1) for j in range(slots)], axis=1
    )
    listed = jnp.broadcast_to(listed.astype(F32), (8, entries)).astype(BF16)
    natural = dot(listed, from_listed)
    transposed = dot(natural.astype(BF16), perm01[...])
    vertex = iota((rows, entries), 0).astype(F32)
    hot0[...] = jnp.where(vertex == transposed[0:1, :], 1.0, 0.0).astype(BF16)
    hot1[...] = jnp.where(vertex == natural[0:1, :], 1.0, 0.0).astype(BF16)
    per_g, per_y = entries // ng, entries // ny
    fetches[2].wait()
    feat = acts[0, x]
    o0[...] = dot(hot0[...], feat[:, :half], TN).astype(BF16).reshape(ng, per_g, half)
    o1[...] = dot(hot1[...], feat[:, half:], TN).astype(BF16).reshape(ny, per_y, half)

    pl.semaphore_wait(barrier, expected)

    out_a0 = Exchange(ng, g, at_g, lambda p: o0.at[p], lambda s, k: a0.at[s], *sem_pair(sem_a0))
    out_a1 = Exchange(ny, y, at_y, lambda p: o1.at[p], lambda s, k: a1.at[s], *sem_pair(sem_a1))
    out_b0 = Exchange(ny, y, at_y, lambda p: s0.at[p], lambda s, k: b0.at[s], *sem_pair(sem_b0))
    out_b1 = Exchange(ng, g, at_g, lambda p: s1.at[p], lambda s, k: b1.at[s], *sem_pair(sem_b1))
    out_a0.start()
    out_a1.start()

    def columns(p):
        return pl.ds(pl.multiple_of(p * width, width), width)

    feats = Exchange(
        nx, x, at_x, lambda p: acts.at[0, x], lambda s, k: acts.at[0, s], *sem_pair(sem_feat)
    )
    cols = Exchange(
        nx, x, at_x, lambda p: weights.at[c, :, columns(p)], lambda s, k: w_cols.at[c, s],
        *sem_pair(sem_cols)
    )
    cols_core = Exchange(
        CORES, c, at_c, lambda p: w_cols.at[c], lambda s, k: w_cols.at[s], *sem_pair(sem_cols_core)
    )
    fetches[3].wait()
    fetches[4].wait()
    cols.start()
    feats.start()
    a0[g] = o0[g]
    a1[y] = o1[y]
    w_cols[c, x] = weights[c, :, columns(x)]

    y_out = lax.div(col, slots * ng)
    g_out = lax.rem(lax.div(col, slots), ng)
    perm10[...] = selection((g_out * ny + y_out) * slots + slot_in)
    for f in fetches[5:]:
        f.wait()

    out_a0.wait_recv()
    s0[...] = dot(perm01[...], a0[...].reshape(entries, half)).astype(BF16).reshape(ny, per_y, half)
    out_b0.start()
    out_a1.wait_recv()
    s1[...] = dot(perm10[...], a1[...].reshape(entries, half)).astype(BF16).reshape(ng, per_g, half)
    out_b1.start()
    b0[y] = s0[y]
    b1[g] = s1[g]

    block_of = tile_dst[...] * src_count + tile_src[...]
    for i in range(dst_count):
        for j in range(src_count):
            here = jnp.where(block_of == i * src_count + j, 1.0, 0.0)
            total = jnp.zeros((tile_rows, tile_rows), F32)
            for t in range(tile_count):
                total += here[:, t : t + 1] * tiles[t].astype(F32)
            top = total.astype(BF16)
            at = (pl.ds(i * tile_rows, tile_rows), pl.ds(j * tile_rows, tile_rows))
            edges[(0,) + at] = top
            edges[(1,) + at] = (total - top.astype(F32)).astype(BF16)
    ones = jnp.ones((rows + entries, tile_rows), BF16)
    degree[...] = jnp.maximum(dot(edges[0], ones) + dot(edges[1], ones), 1.0)
    for i in range(2):
        edges_t[i] = dot(edges[i, :, rows:], perm01[...]).astype(BF16)
    own_sum[...] = dot(edges[0, :, :rows], feat) + dot(edges[1, :, :rows], feat)
    cols.wait_recv()
    cols_core.start()

    safe = jnp.concatenate([degree[...]] * (width // tile_rows), axis=1)
    out_b0.wait_recv()
    mirrored = b0[...].reshape(entries, half)
    left = dot(edges[0, :, rows:], mirrored) + dot(edges[1, :, rows:], mirrored)
    acts[1, x, :, :half] = ((own_sum[:, :half] + left) / safe[:, :half]).astype(BF16)
    out_b1.wait_recv()
    mirrored = b1[...].reshape(entries, half)
    right = dot(edges_t[0], mirrored) + dot(edges_t[1], mirrored)
    acts[1, x, :, half:] = ((own_sum[:, half:] + right) / safe[:, half:]).astype(BF16)
    aggs = Exchange(
        nx, x, at_x, lambda p: acts.at[1, x], lambda s, k: acts.at[1, s], *sem_pair(sem_agg)
    )
    aggs.start()

    def pass_acts(k):
        q = lax.rem(x - k + nx, nx)
        return Exchange(
            CORES, c, at_c, lambda p: acts.at[p, q], lambda s, i: acts_peer.at[q],
            *(sem.at[pl.ds(k, 1)] for sem in sem_pair(sem_acts))
        )

    feats.wait_recv()
    send_acts = [pass_acts(k) for k in range(nx)]
    send_acts[0].start()
    cols_core.wait_recv()
    total = dot(acts[1, x], w_cols[1, x])
    for q in range(nx):
        total += dot(acts[0, q], w_cols[0, q])
    pre_act[...] = total
    for k in range(1, nx):
        q = lax.rem(x - k + nx, nx)
        aggs.wait_recv_one(k)
        send_acts[k].start()
        pre_act[...] += dot(acts[1, q], w_cols[1, q])
    value = pre_act[...]
    sig = jax.nn.sigmoid(value)
    grads[x] = (grad_out[...].astype(F32) * (sig + value * sig * (1.0 - sig))).astype(BF16)

    send_grads = Exchange(
        CORES, c, at_c, lambda p: grads.at[x], lambda s, k: grads_peer, *sem_pair(sem_pass)
    )
    gather = Exchange(
        nx, x, at_x, lambda p: grads.at[x], lambda s, k: grads.at[s], *sem_pair(sem_gather)
    )
    send_grads.start()
    gather.start()
    hidden[...] = (value * sig).astype(BF16)

    for q in range(nx):
        w_acc[q] = dot(acts[c, q], grads[x], TN)
    for done in send_acts:
        done.wait_recv()
    send_grads.wait_recv()
    for q in range(nx):
        block = (w_acc[q] + dot(acts_peer[q], grads_peer[...], TN)).astype(BF16)
        for h in range(2):
            wa_send[h, :, q] = block[h * half : (h + 1) * half, :].reshape(ny, band, width)

    def first(h):
        way = ways[h]
        return Exchange(
            way["n"], way["me"], way["at"], lambda p: wa_send.at[h, p],
            lambda s, k: wa_recv.at[h, k - 1], *sem_pair(sem_first, h)
        )

    firsts = [first(0), first(1)]
    for way in firsts:
        way.start()

    direct[...] = dot(grads[x], weights[0, :, columns(x)], NT)
    grad_agg[...] = dot(grads[x], weights[1, :, columns(x)], NT)
    for k in range(1, nx):
        q = lax.rem(x - k + nx, nx)
        gather.wait_recv_one(k)
        direct[...] += dot(grads[q], weights[0, :, columns(q)], NT)
        grad_agg[...] += dot(grads[q], weights[1, :, columns(q)], NT)
    scaled = (grad_agg[...] / safe).astype(BF16)
    left, right = scaled[:, :half], scaled[:, half:]
    left = dot(edges[0, :, rows:], left, TN) + dot(edges[1, :, rows:], left, TN)
    right = dot(edges_t[0], right, TN) + dot(edges_t[1], right, TN)
    c0[...] = left.astype(BF16).reshape(ny, per_y, half)
    c1[...] = right.astype(BF16).reshape(ng, per_g, half)
    back_d0 = Exchange(ny, y, at_y, lambda p: c0.at[p], lambda s, k: d0.at[s], *sem_pair(sem_d0))
    back_d1 = Exchange(ng, g, at_g, lambda p: c1.at[p], lambda s, k: d1.at[s], *sem_pair(sem_d1))
    back_f0 = Exchange(ng, g, at_g, lambda p: e0.at[p], lambda s, k: f0.at[s], *sem_pair(sem_f0))
    back_f1 = Exchange(ny, y, at_y, lambda p: e1.at[p], lambda s, k: f1.at[s], *sem_pair(sem_f1))
    back_d0.start()
    back_d1.start()
    d0[y] = c0[y]
    d1[g] = c1[g]

    def second(h):
        way = ways[1 - h]
        return Exchange(
            way["n"], way["me"], way["at"], lambda p: wb_send.at[h, p],
            lambda s, k: wb_recv.at[h, k - 1], *sem_pair(sem_second, h)
        )

    seconds = [second(0), second(1)]
    for h in range(2):
        firsts[h].wait_recv()
        way, after = ways[h], ways[1 - h]
        for q in range(nx):
            total = wa_send[h, way["me"], q].astype(F32)
            for k in range(way["n"] - 1):
                total = total + wa_recv[h, k, q].astype(F32)
            for i in range(parts):
                wb_send[h, q * parts + i] = total[:, i * piece : (i + 1) * piece]
        seconds[h].start()

    direct[...] += dot(edges[0, :, :rows], scaled, TN) + dot(edges[1, :, :rows], scaled, TN)

    scale = float(rows * nd) ** (-0.5)

    def piece_at(h, i, column):
        r = h * half + ways[h]["me"] * band
        q = column * width + lax.rem(i, parts) * piece
        return out_w.at[c, pl.ds(pl.multiple_of(r, band), band), pl.ds(pl.multiple_of(q, piece), piece)]

    def third(h, k, dst, device, slot):
        return pltpu.make_async_remote_copy(
            src_ref=wt_send.at[h], dst_ref=dst, send_sem=sem_third.at[h, 0, k],
            recv_sem=sem_third.at[h, 1, slot], device_id=device, device_id_type=MESH,
        )

    def thirds(h, step):
        after = ways[1 - h]
        me = after["me"]
        slot = lax.rem(me, parts) * nx + x
        target = lax.div(me, parts)

        def one(j, carry):
            k = far_first(after["n"], j)
            copy = third(h, k, piece_at(h, me, x), across(h, lax.rem(me + k, after["n"]), target), slot)

            @pl.when(jnp.logical_or(k != 0, target != x))
            def _():
                step(copy)

            return carry

        lax.fori_loop(0, after["n"], one, 0)

    for h in range(2):
        seconds[h].wait_recv()
        after = ways[1 - h]
        total = wb_send[h, after["me"]]
        for k in range(after["n"] - 1):
            total = total + wb_recv[h, k]
        wt_send[h] = (total * scale).astype(BF16)
        thirds(h, lambda copy: copy.start())

        @pl.when(lax.div(after["me"], parts) == x)
        def _():
            piece_at(h, after["me"], x)[...] = wt_send[h]

    back_d0.wait_recv()
    e0[...] = dot(perm10[...], d0[...].reshape(entries, half)).astype(BF16).reshape(ng, per_g, half)
    back_f0.start()
    back_d1.wait_recv()
    e1[...] = dot(perm01[...], d1[...].reshape(entries, half)).astype(BF16).reshape(ny, per_y, half)
    back_f1.start()
    f0[g] = e0[g]
    f1[y] = e1[y]

    def band_at(h, i, core):
        return out_w.at[core, pl.ds(pl.multiple_of(h * half + i * band, band), band), :]

    def fourth(h):
        way = ways[h]
        return Exchange(
            way["n"], way["me"], way["at"], lambda p: band_at(h, way["me"], c),
            lambda s, k: band_at(h, s, c), *sem_pair(sem_fourth, h)
        )

    def swap(h, k):
        way = ways[h]
        i = lax.rem(way["me"] - k + way["n"], way["n"])
        return pltpu.make_async_remote_copy(
            src_ref=band_at(h, i, c), dst_ref=band_at(h, i, c), send_sem=sem_swap.at[h, 0, k],
            recv_sem=sem_swap.at[h, 1, k], device_id=at_c(1 - c), device_id_type=MESH,
        )

    fourths = [fourth(0), fourth(1)]
    for h in range(2):
        senders(
            h,
            lambda k, i, column: third(h, 0, piece_at(h, i, column), across(h, i, column), k).wait_recv(),
        )
        fourths[h].start()
        swap(h, 0).start()

    def pass_on(k):
        for h in range(2):
            fourths[h].wait_recv_one(k)
            swap(h, k).start()

    fourths[0].each(pass_on)

    back_f0.wait_recv()
    grad_feat[:, :half] = (
        direct[:, :half] + dot(hot0[...], f0[...].reshape(entries, half))
    ).astype(BF16)
    back_f1.wait_recv()
    grad_feat[:, half:] = (
        direct[:, half:] + dot(hot1[...], f1[...].reshape(entries, half))
    ).astype(BF16)

    def swapped(k, carry):
        for h in range(2):
            swap(h, k).wait_recv()
            swap(h, k).wait_send()
        return carry

    lax.fori_loop(0, ny, swapped, 0)
    for h in range(2):
        thirds(h, lambda copy: copy.wait_send())
    for done in (
        [out_a0, out_a1, out_b0, out_b1, feats, cols, cols_core, aggs, send_grads]
        + [gather, back_d0, back_d1, back_f0, back_f1] + send_acts + firsts + seconds + fourths
    ):
        done.wait_send()


def write_out(hidden, grad_feat, both, out0, out1, out2, out3, sem):
    pairs = ((hidden, out0), (grad_feat, out1), (both.at[0], out2), (both.at[1], out3))
    copies = [pltpu.make_async_copy(src, dst, sem.at[i]) for i, (src, dst) in enumerate(pairs)]
    for copy in copies:
        copy.start()
    for copy in copies:
        copy.wait()


def sem_pair(sems, use=0):
    return sems.at[use, 0], sems.at[use, 1]


def solution(mesh):
    doms, nx = mesh.shape["dom"], mesh.shape["rep"]
    ny, nz = GRIDS[doms]
    ng = nz * CORES

    def local(
        features, w_self, w_neigh, grad_out, mirror_list, mirror_count, tile_dst, tile_src, tiles
    ):
        rows, width = features.shape
        half, full = width // 2, width * nx
        slots = mirror_list.shape[1]
        entries = doms * slots
        tile_count, tile_rows = tiles.shape[0], tiles.shape[1]
        per_g, per_y = entries // ng, entries // ny
        assert ny == nz and rows == width and nz % nx == 0
        parts = nz // nx
        band, piece = half // ny, width // parts
        vmem, stay = (pl.BlockSpec(memory_space=s) for s in (pltpu.VMEM, pl.ANY))

        def scratch(*shape, kind=BF16):
            return pltpu.VMEM(shape, kind)

        def sems(n, uses=1):
            return pltpu.SemaphoreType.DMA((uses, 2, n))

        by_g, by_y = scratch(ng, per_g, half), scratch(ny, per_y, half)
        buffers = [
            scratch(2, width, full), scratch(rows, width),
            scratch(slots, doms, kind=jnp.int32), scratch(1, doms, kind=jnp.int32),
            scratch(1, tile_count, kind=jnp.int32), scratch(1, tile_count, kind=jnp.int32),
            scratch(tile_count, tile_rows, tile_rows),
            scratch(entries, entries), scratch(entries, entries),
            scratch(rows, entries), scratch(rows, entries),
            scratch(2, rows, rows + entries), scratch(2, rows, entries),
            scratch(rows, tile_rows, kind=F32),
            scratch(rows, width, kind=F32),
            by_g, by_g, by_y, by_y, by_y, by_y, by_g, by_g,
            scratch(2, nx, rows, width), scratch(nx, rows, width), scratch(2, nx, width, width),
            scratch(rows, width, kind=F32), scratch(nx, rows, width), scratch(rows, width),
            scratch(rows, width, kind=F32), scratch(rows, width, kind=F32),
            by_y, by_y, by_g, by_g, by_g, by_g, by_y, by_y,
            scratch(nx, width, width, kind=F32),
            scratch(2, ny, nx, band, width), scratch(2, ny - 1, nx, band, width),
            scratch(2, nz, band, piece, kind=F32), scratch(2, nz - 1, band, piece, kind=F32),
            scratch(2, band, piece),
        ]
        semaphores = [
            pltpu.SemaphoreType.DMA((9,)),
            sems(ng - 1), sems(ny - 1), sems(ny - 1), sems(ng - 1),
            sems(nx - 1), sems(nx - 1), sems(1), sems(nx - 1), sems(nx),
            sems(nx - 1), sems(1), sems(ny - 1), sems(ng - 1), sems(ng - 1), sems(ny - 1),
            sems(ny - 1, 2), sems(ny - 1, 2), sems(nz, 2), sems(ny - 1, 2), sems(ny, 2),
        ]
        shapes = (
            jax.ShapeDtypeStruct((rows, width), BF16),
            jax.ShapeDtypeStruct((rows, width), BF16),
            jax.ShapeDtypeStruct((2, width, full), BF16),
        )
        results = pl.pallas_call(
            functools.partial(kernel, (ny, nz, nx)),
            out_shape=tuple(pltpu.VMEM(v.shape, v.dtype) for v in shapes),
            in_specs=[pl.BlockSpec(memory_space=pltpu.HBM)] * 9,
            out_specs=(vmem, vmem, vmem),
            scratch_shapes=buffers + semaphores,
            compiler_params=pltpu.CompilerParams(
                collective_id=0, has_side_effects=True, vmem_limit_bytes=32 * 2**20
            ),
        )(
            *(
                pltpu.with_memory_space_constraint(v, pltpu.HBM)
                for v in (
                    features, w_self, w_neigh, grad_out, mirror_list.T, mirror_count[None, :],
                    tile_dst[None, :], tile_src[None, :], tiles,
                )
            )
        )
        weight = jax.ShapeDtypeStruct((width, full), BF16)
        return pl.pallas_call(
            write_out,
            out_shape=shapes[:2] + (weight, weight),
            in_specs=[vmem] * 3,
            out_specs=(stay,) * 4,
            scratch_shapes=[pltpu.SemaphoreType.DMA((4,))],
        )(*(pltpu.with_memory_space_constraint(v, pltpu.VMEM) for v in results))

    in_specs = (
        P("dom", "rep"),
        P("rep", None),
        P("rep", None),
        P("dom", "rep"),
        P("dom", None),
        P("dom"),
        P("dom"),
        P("dom"),
        P("dom", None, None),
    )
    out_specs = (P("dom", "rep"), P("dom", "rep"), P("rep", None), P("rep", None))
    return jax.shard_map(local, mesh=mesh, in_specs=in_specs, out_specs=out_specs, check_vma=False)
```

```python
import functools

import jax
import jax.numpy as jnp
from jax import lax
from jax.experimental import pallas as pl
from jax.experimental.pallas import tpu as pltpu
from jax.sharding import PartitionSpec as P

MESH = pl.DeviceIdType.MESH
F32 = jnp.float32
BF16 = jnp.bfloat16
CORES = 2
GRIDS = {128: (8, 8), 8: (2, 2)}

NN = (((1,), (0,)), ((), ()))
TN = (((0,), (0,)), ((), ()))
NT = (((1,), (1,)), ((), ()))


def dot(a, b, dims=NN):
    return lax.dot_general(a, b, dims, preferred_element_type=F32)


def far_first(n):
    return sorted(range(1, n), key=lambda k: -min(k, n - k))


class Exchange:
    def __init__(self, n, me, device, src, dst, send_sem, recv_sem):
        self.n, self.me, self.device = n, me, device
        self.src, self.dst = src, dst
        self.send_sem, self.recv_sem = send_sem, recv_sem

    def copy(self, k, src, dst, peer):
        return pltpu.make_async_remote_copy(
            src_ref=src,
            dst_ref=dst,
            send_sem=self.send_sem.at[k - 1],
            recv_sem=self.recv_sem.at[k - 1],
            device_id=self.device(peer),
            device_id_type=MESH,
        )

    def each(self, step):
        for k in reversed(far_first(self.n)):
            step(k)

    def outgoing(self, k):
        peer = lax.rem(self.me + k, self.n)
        return self.copy(k, self.src(peer), self.dst(self.me, k), peer)

    def start(self):
        for k in far_first(self.n):
            self.outgoing(k).start()

    def wait_send(self):
        self.each(lambda k: self.outgoing(k).wait_send())

    def wait_recv_one(self, k):
        peer = lax.rem(self.me - k + self.n, self.n)
        slot = self.dst(peer, k)
        self.copy(k, slot, slot, peer).wait_recv()

    def wait_recv(self):
        self.each(self.wait_recv_one)


def kernel(
    dims,
    feat_in, w_self_in, w_neigh_in, grad_out_in, list_in, count_in, dst_in, src_in, tiles_in,
    hidden, grad_feat, out_w,
    weights, grad_out, list_t, count, tile_dst, tile_src, tiles,
    perm01, perm10, hot0, hot1, edges, edges_t, degree, own_sum,
    o0, a0, s0, b0, o1, a1, s1, b1,
    acts, acts_peer, w_cols, pre_act, grads, grads_peer, direct, grad_agg,
    c0, d0, e0, f0, c1, d1, e1, f1,
    w_acc, wa_send, wa_recv, wb_send, wb_recv, wt_send,
    in_sem,
    sem_a0, sem_a1, sem_b0, sem_b1, sem_feat, sem_cols, sem_cols_core, sem_agg, sem_acts,
    sem_gather, sem_pass, sem_d0, sem_d1, sem_f0, sem_f1, sem_first, sem_second,
    sem_third, sem_fourth, sem_swap,
):
    ny, nz, nx = dims
    ng = nz * CORES
    nd = ny * ng
    rows, width = feat_in.shape
    half = width // 2
    slots = list_in.shape[0]
    entries = nd * slots
    tile_count, tile_rows = tiles_in.shape[0], tiles_in.shape[1]
    dst_count = rows // tile_rows
    src_count = (rows + entries) // tile_rows
    parts = nz // nx
    band, piece = half // ny, width // parts

    dom = lax.axis_index("dom")
    x = lax.axis_index("rep")
    y = lax.div(dom, ng)
    g = lax.rem(dom, ng)
    z = lax.div(g, CORES)
    c = lax.rem(g, CORES)

    def at_g(peer):
        return (y * ng + peer, x)

    def at_y(peer):
        return (peer * ng + g, x)

    def at_z(peer):
        return (y * ng + peer * CORES + c, x)

    def at_c(peer):
        return (y * ng + z * CORES + peer, x)

    def at_x(peer):
        return (dom, peer)

    def fetch(i, src, dst):
        return pltpu.make_async_copy(src, dst, in_sem.at[i])

    fetches = [
        fetch(0, list_in, list_t),
        fetch(1, count_in, count),
        fetch(2, feat_in, acts.at[0, x]),
        fetch(3, w_self_in, weights.at[0]),
        fetch(4, w_neigh_in, weights.at[1]),
        fetch(5, dst_in, tile_dst),
        fetch(6, src_in, tile_src),
        fetch(7, tiles_in, tiles),
        fetch(8, grad_out_in, grad_out),
    ]
    barrier = pltpu.get_barrier_semaphore()

    def greet_one(device):
        pl.semaphore_signal(barrier, inc=1, device_id=device, device_id_type=MESH)

    def greet(n, me, device):
        for k in far_first(n):
            greet_one(device(lax.rem(me + k, n)))

    greet(ny, y, at_y)
    greet(ng, g, at_g)
    greet(nx, x, at_x)

    ways = (dict(n=ny, me=y, at=at_y), dict(n=nz, me=z, at=at_z))

    def across(h, i, column):
        return (ways[1 - h]["at"](i)[0], column)

    def senders(h, step):
        def one(k):
            i, column = x * parts + k // nx, k % nx

            @pl.when(jnp.logical_or(i != ways[1 - h]["me"], column != x))
            def _():
                step(k, i, column)

        for k in range(parts * nx):
            one(k)

    expected = (ng - 1) + (ny - 1) + (nx - 1)
    for f in fetches:
        f.start()

    def iota(shape, axis):
        return lax.broadcasted_iota(jnp.int32, shape, axis)

    col = iota((1, entries), 1)
    row = iota((entries, entries), 0)

    def selection(index):
        return jnp.where(row == index, 1.0, 0.0).astype(BF16)

    from_listed = selection(lax.rem(col, slots) * nd + lax.div(col, slots))
    y_in = lax.rem(lax.div(col, slots), ny)
    g_in = lax.div(col, slots * ny)
    slot_in = lax.rem(col, slots)
    perm01[...] = selection((y_in * ng + g_in) * slots + slot_in)

    fetches[0].wait()
    fetches[1].wait()
    listed = jnp.concatenate(
        [jnp.where(j < count[...], list_t[j : j + 1, :], -1) for j in range(slots)], axis=1
    )
    listed = jnp.broadcast_to(listed.astype(F32), (8, entries)).astype(BF16)
    natural = dot(listed, from_listed)
    transposed = dot(natural.astype(BF16), perm01[...])
    vertex = iota((rows, entries), 0).astype(F32)
    hot0[...] = jnp.where(vertex == transposed[0:1, :], 1.0, 0.0).astype(BF16)
    hot1[...] = jnp.where(vertex == natural[0:1, :], 1.0, 0.0).astype(BF16)
    per_g, per_y = entries // ng, entries // ny
    fetches[2].wait()
    feat = acts[0, x]
    o0[...] = dot(hot0[...], feat[:, :half], TN).astype(BF16).reshape(ng, per_g, half)
    o1[...] = dot(hot1[...], feat[:, half:], TN).astype(BF16).reshape(ny, per_y, half)

    pl.semaphore_wait(barrier, expected)

    out_a0 = Exchange(ng, g, at_g, lambda p: o0.at[p], lambda s, k: a0.at[s], *sem_pair(sem_a0))
    out_a1 = Exchange(ny, y, at_y, lambda p: o1.at[p], lambda s, k: a1.at[s], *sem_pair(sem_a1))
    out_b0 = Exchange(ny, y, at_y, lambda p: s0.at[p], lambda s, k: b0.at[s], *sem_pair(sem_b0))
    out_b1 = Exchange(ng, g, at_g, lambda p: s1.at[p], lambda s, k: b1.at[s], *sem_pair(sem_b1))
    out_a0.start()
    out_a1.start()

    def columns(p):
        return pl.ds(pl.multiple_of(p * width, width), width)

    feats = Exchange(
        nx, x, at_x, lambda p: acts.at[0, x], lambda s, k: acts.at[0, s], *sem_pair(sem_feat)
    )
    cols = Exchange(
        nx, x, at_x, lambda p: weights.at[c, :, columns(p)], lambda s, k: w_cols.at[c, s],
        *sem_pair(sem_cols)
    )
    cols_core = Exchange(
        CORES, c, at_c, lambda p: w_cols.at[c], lambda s, k: w_cols.at[s], *sem_pair(sem_cols_core)
    )
    fetches[3].wait()
    fetches[4].wait()
    cols.start()
    feats.start()
    a0[g] = o0[g]
    a1[y] = o1[y]
    w_cols[c, x] = weights[c, :, columns(x)]

    y_out = lax.div(col, slots * ng)
    g_out = lax.rem(lax.div(col, slots), ng)
    perm10[...] = selection((g_out * ny + y_out) * slots + slot_in)
    for f in fetches[5:]:
        f.wait()

    out_a0.wait_recv()
    s0[...] = dot(perm01[...], a0[...].reshape(entries, half)).astype(BF16).reshape(ny, per_y, half)
    out_b0.start()
    out_a1.wait_recv()
    s1[...] = dot(perm10[...], a1[...].reshape(entries, half)).astype(BF16).reshape(ng, per_g, half)
    out_b1.start()
    b0[y] = s0[y]
    b1[g] = s1[g]

    block_of = tile_dst[...] * src_count + tile_src[...]
    for i in range(dst_count):
        for j in range(src_count):
            here = jnp.where(block_of == i * src_count + j, 1.0, 0.0)
            total = jnp.zeros((tile_rows, tile_rows), F32)
            for t in range(tile_count):
                total += here[:, t : t + 1] * tiles[t].astype(F32)
            top = total.astype(BF16)
            at = (pl.ds(i * tile_rows, tile_rows), pl.ds(j * tile_rows, tile_rows))
            edges[(0,) + at] = top
            edges[(1,) + at] = (total - top.astype(F32)).astype(BF16)
    ones = jnp.ones((rows + entries, tile_rows), BF16)
    degree[...] = jnp.maximum(dot(edges[0], ones) + dot(edges[1], ones), 1.0)
    for i in range(2):
        edges_t[i] = dot(edges[i, :, rows:], perm01[...]).astype(BF16)
    own_sum[...] = dot(edges[0, :, :rows], feat) + dot(edges[1, :, :rows], feat)
    cols.wait_recv()
    cols_core.start()

    safe = jnp.concatenate([degree[...]] * (width // tile_rows), axis=1)
    def gather_mean(h):
        here = pl.ds(h * half, half)
        return Exchange(
            nx, x, at_x, lambda p: acts.at[1, x, :, here], lambda s, k: acts.at[1, s, :, here],
            *sem_pair(sem_agg, h)
        )

    aggs = [gather_mean(0), gather_mean(1)]
    out_b0.wait_recv()
    mirrored = b0[...].reshape(entries, half)
    left = dot(edges[0, :, rows:], mirrored) + dot(edges[1, :, rows:], mirrored)
    acts[1, x, :, :half] = ((own_sum[:, :half] + left) / safe[:, :half]).astype(BF16)
    aggs[0].start()
    out_b1.wait_recv()
    mirrored = b1[...].reshape(entries, half)
    right = dot(edges_t[0], mirrored) + dot(edges_t[1], mirrored)
    acts[1, x, :, half:] = ((own_sum[:, half:] + right) / safe[:, half:]).astype(BF16)
    aggs[1].start()

    def pass_acts(k):
        q = lax.rem(x - k + nx, nx)
        return Exchange(
            CORES, c, at_c, lambda p: acts.at[p, q], lambda s, i: acts_peer.at[q],
            *(sem.at[pl.ds(k, 1)] for sem in sem_pair(sem_acts))
        )

    feats.wait_recv()
    send_acts = [pass_acts(k) for k in range(nx)]
    send_acts[0].start()
    cols_core.wait_recv()
    total = dot(acts[1, x], w_cols[1, x])
    for q in range(nx):
        total += dot(acts[0, q], w_cols[0, q])
    pre_act[...] = total
    for k in range(1, nx):
        q = lax.rem(x - k + nx, nx)
        aggs[0].wait_recv_one(k)
        aggs[1].wait_recv_one(k)
        send_acts[k].start()
        pre_act[...] += dot(acts[1, q], w_cols[1, q])
    value = pre_act[...]
    sig = jax.nn.sigmoid(value)
    grads[x] = (grad_out[...].astype(F32) * (sig + value * sig * (1.0 - sig))).astype(BF16)

    send_grads = Exchange(
        CORES, c, at_c, lambda p: grads.at[x], lambda s, k: grads_peer, *sem_pair(sem_pass)
    )
    gather = Exchange(
        nx, x, at_x, lambda p: grads.at[x], lambda s, k: grads.at[s], *sem_pair(sem_gather)
    )
    send_grads.start()
    gather.start()
    hidden[...] = (value * sig).astype(BF16)

    for q in range(nx):
        w_acc[q] = dot(acts[c, q], grads[x], TN)
    for done in send_acts:
        done.wait_recv()
    send_grads.wait_recv()
    for q in range(nx):
        block = (w_acc[q] + dot(acts_peer[q], grads_peer[...], TN)).astype(BF16)
        for h in range(2):
            wa_send[h, :, q] = block[h * half : (h + 1) * half, :].reshape(ny, band, width)

    def first(h):
        way = ways[h]
        return Exchange(
            way["n"], way["me"], way["at"], lambda p: wa_send.at[h, p],
            lambda s, k: wa_recv.at[h, k - 1], *sem_pair(sem_first, h)
        )

    firsts = [first(0), first(1)]
    for way in firsts:
        way.start()

    direct[...] = dot(grads[x], weights[0, :, columns(x)], NT)
    grad_agg[...] = dot(grads[x], weights[1, :, columns(x)], NT)
    for k in range(1, nx):
        q = lax.rem(x - k + nx, nx)
        gather.wait_recv_one(k)
        direct[...] += dot(grads[q], weights[0, :, columns(q)], NT)
        grad_agg[...] += dot(grads[q], weights[1, :, columns(q)], NT)
    scaled = (grad_agg[...] / safe).astype(BF16)
    left, right = scaled[:, :half], scaled[:, half:]
    left = dot(edges[0, :, rows:], left, TN) + dot(edges[1, :, rows:], left, TN)
    right = dot(edges_t[0], right, TN) + dot(edges_t[1], right, TN)
    c0[...] = left.astype(BF16).reshape(ny, per_y, half)
    c1[...] = right.astype(BF16).reshape(ng, per_g, half)
    back_d0 = Exchange(ny, y, at_y, lambda p: c0.at[p], lambda s, k: d0.at[s], *sem_pair(sem_d0))
    back_d1 = Exchange(ng, g, at_g, lambda p: c1.at[p], lambda s, k: d1.at[s], *sem_pair(sem_d1))
    back_f0 = Exchange(ng, g, at_g, lambda p: e0.at[p], lambda s, k: f0.at[s], *sem_pair(sem_f0))
    back_f1 = Exchange(ny, y, at_y, lambda p: e1.at[p], lambda s, k: f1.at[s], *sem_pair(sem_f1))
    back_d0.start()
    back_d1.start()
    d0[y] = c0[y]
    d1[g] = c1[g]

    def second(h):
        way = ways[1 - h]
        return Exchange(
            way["n"], way["me"], way["at"], lambda p: wb_send.at[h, p],
            lambda s, k: wb_recv.at[h, k - 1], *sem_pair(sem_second, h)
        )

    seconds = [second(0), second(1)]
    for h in range(2):
        firsts[h].wait_recv()
        way, after = ways[h], ways[1 - h]
        for q in range(nx):
            total = wa_send[h, way["me"], q].astype(F32)
            for k in range(way["n"] - 1):
                total = total + wa_recv[h, k, q].astype(F32)
            for i in range(parts):
                wb_send[h, q * parts + i] = total[:, i * piece : (i + 1) * piece]
        seconds[h].start()

    direct[...] += dot(edges[0, :, :rows], scaled, TN) + dot(edges[1, :, :rows], scaled, TN)

    scale = float(rows * nd) ** (-0.5)

    def piece_at(h, i, column):
        r = h * half + ways[h]["me"] * band
        q = column * width + lax.rem(i, parts) * piece
        return out_w.at[c, pl.ds(pl.multiple_of(r, band), band), pl.ds(pl.multiple_of(q, piece), piece)]

    def third(h, k, dst, device, slot):
        return pltpu.make_async_remote_copy(
            src_ref=wt_send.at[h], dst_ref=dst, send_sem=sem_third.at[h, 0, k],
            recv_sem=sem_third.at[h, 1, slot], device_id=device, device_id_type=MESH,
        )

    def thirds(h, step):
        after = ways[1 - h]
        me = after["me"]
        slot = lax.rem(me, parts) * nx + x
        target = lax.div(me, parts)

        def one(k):
            copy = third(h, k, piece_at(h, me, x), across(h, lax.rem(me + k, after["n"]), target), slot)

            if k != 0:
                step(copy)
            else:
                pl.when(target != x)(lambda: step(copy))

        for k in far_first(after["n"]) + [0]:
            one(k)

    for h in range(2):
        seconds[h].wait_recv()
        after = ways[1 - h]
        total = wb_send[h, after["me"]]
        for k in range(after["n"] - 1):
            total = total + wb_recv[h, k]
        wt_send[h] = (total * scale).astype(BF16)
        thirds(h, lambda copy: copy.start())

        @pl.when(lax.div(after["me"], parts) == x)
        def _():
            piece_at(h, after["me"], x)[...] = wt_send[h]

    back_d0.wait_recv()
    e0[...] = dot(perm10[...], d0[...].reshape(entries, half)).astype(BF16).reshape(ng, per_g, half)
    back_f0.start()
    back_d1.wait_recv()
    e1[...] = dot(perm01[...], d1[...].reshape(entries, half)).astype(BF16).reshape(ny, per_y, half)
    back_f1.start()
    f0[g] = e0[g]
    f1[y] = e1[y]

    def band_at(h, i, core):
        return out_w.at[core, pl.ds(pl.multiple_of(h * half + i * band, band), band), :]

    def fourth(h):
        way = ways[h]
        return Exchange(
            way["n"], way["me"], way["at"], lambda p: band_at(h, way["me"], c),
            lambda s, k: band_at(h, s, c), *sem_pair(sem_fourth, h)
        )

    def swap(h, k):
        way = ways[h]
        i = lax.rem(way["me"] - k + way["n"], way["n"])
        return pltpu.make_async_remote_copy(
            src_ref=band_at(h, i, c), dst_ref=band_at(h, i, c), send_sem=sem_swap.at[h, 0, k],
            recv_sem=sem_swap.at[h, 1, k], device_id=at_c(1 - c), device_id_type=MESH,
        )

    fourths = [fourth(0), fourth(1)]
    for h in range(2):
        senders(
            h,
            lambda k, i, column: third(h, 0, piece_at(h, i, column), across(h, i, column), k).wait_recv(),
        )
        fourths[h].start()
        swap(h, 0).start()

    def pass_on(k):
        for h in range(2):
            fourths[h].wait_recv_one(k)
            swap(h, k).start()

    fourths[0].each(pass_on)

    back_f0.wait_recv()
    grad_feat[:, :half] = (
        direct[:, :half] + dot(hot0[...], f0[...].reshape(entries, half))
    ).astype(BF16)
    back_f1.wait_recv()
    grad_feat[:, half:] = (
        direct[:, half:] + dot(hot1[...], f1[...].reshape(entries, half))
    ).astype(BF16)

    for k in range(ny):
        for h in range(2):
            swap(h, k).wait_recv()
            swap(h, k).wait_send()
    for h in range(2):
        thirds(h, lambda copy: copy.wait_send())
    for done in (
        [out_a0, out_a1, out_b0, out_b1, feats, cols, cols_core, send_grads]
        + [gather, back_d0, back_d1, back_f0, back_f1] + aggs + send_acts + firsts + seconds + fourths
    ):
        done.wait_send()


def write_out(hidden, grad_feat, both, out0, out1, out2, out3, sem):
    pairs = ((hidden, out0), (grad_feat, out1), (both.at[0], out2), (both.at[1], out3))
    copies = [pltpu.make_async_copy(src, dst, sem.at[i]) for i, (src, dst) in enumerate(pairs)]
    for copy in copies:
        copy.start()
    for copy in copies:
        copy.wait()


def sem_pair(sems, use=0):
    return sems.at[use, 0], sems.at[use, 1]


def solution(mesh):
    doms, nx = mesh.shape["dom"], mesh.shape["rep"]
    ny, nz = GRIDS[doms]
    ng = nz * CORES

    def local(
        features, w_self, w_neigh, grad_out, mirror_list, mirror_count, tile_dst, tile_src, tiles
    ):
        rows, width = features.shape
        half, full = width // 2, width * nx
        slots = mirror_list.shape[1]
        entries = doms * slots
        tile_count, tile_rows = tiles.shape[0], tiles.shape[1]
        per_g, per_y = entries // ng, entries // ny
        assert ny == nz and rows == width and nz % nx == 0
        parts = nz // nx
        band, piece = half // ny, width // parts
        vmem, stay = (pl.BlockSpec(memory_space=s) for s in (pltpu.VMEM, pl.ANY))

        def scratch(*shape, kind=BF16):
            return pltpu.VMEM(shape, kind)

        def sems(n, uses=1):
            return pltpu.SemaphoreType.DMA((uses, 2, n))

        by_g, by_y = scratch(ng, per_g, half), scratch(ny, per_y, half)
        buffers = [
            scratch(2, width, full), scratch(rows, width),
            scratch(slots, doms, kind=jnp.int32), scratch(1, doms, kind=jnp.int32),
            scratch(1, tile_count, kind=jnp.int32), scratch(1, tile_count, kind=jnp.int32),
            scratch(tile_count, tile_rows, tile_rows),
            scratch(entries, entries), scratch(entries, entries),
            scratch(rows, entries), scratch(rows, entries),
            scratch(2, rows, rows + entries), scratch(2, rows, entries),
            scratch(rows, tile_rows, kind=F32),
            scratch(rows, width, kind=F32),
            by_g, by_g, by_y, by_y, by_y, by_y, by_g, by_g,
            scratch(2, nx, rows, width), scratch(nx, rows, width), scratch(2, nx, width, width),
            scratch(rows, width, kind=F32), scratch(nx, rows, width), scratch(rows, width),
            scratch(rows, width, kind=F32), scratch(rows, width, kind=F32),
            by_y, by_y, by_g, by_g, by_g, by_g, by_y, by_y,
            scratch(nx, width, width, kind=F32),
            scratch(2, ny, nx, band, width), scratch(2, ny - 1, nx, band, width),
            scratch(2, nz, band, piece, kind=F32), scratch(2, nz - 1, band, piece, kind=F32),
            scratch(2, band, piece),
        ]
        semaphores = [
            pltpu.SemaphoreType.DMA((9,)),
            sems(ng - 1), sems(ny - 1), sems(ny - 1), sems(ng - 1),
            sems(nx - 1), sems(nx - 1), sems(1), sems(nx - 1, 2), sems(nx),
            sems(nx - 1), sems(1), sems(ny - 1), sems(ng - 1), sems(ng - 1), sems(ny - 1),
            sems(ny - 1, 2), sems(ny - 1, 2), sems(nz, 2), sems(ny - 1, 2), sems(ny, 2),
        ]
        shapes = (
            jax.ShapeDtypeStruct((rows, width), BF16),
            jax.ShapeDtypeStruct((rows, width), BF16),
            jax.ShapeDtypeStruct((2, width, full), BF16),
        )
        results = pl.pallas_call(
            functools.partial(kernel, (ny, nz, nx)),
            out_shape=tuple(pltpu.VMEM(v.shape, v.dtype) for v in shapes),
            in_specs=[pl.BlockSpec(memory_space=pltpu.HBM)] * 9,
            out_specs=(vmem, vmem, vmem),
            scratch_shapes=buffers + semaphores,
            compiler_params=pltpu.CompilerParams(
                collective_id=0, has_side_effects=True, vmem_limit_bytes=32 * 2**20
            ),
        )(
            *(
                pltpu.with_memory_space_constraint(v, pltpu.HBM)
                for v in (
                    features, w_self, w_neigh, grad_out, mirror_list.T, mirror_count[None, :],
                    tile_dst[None, :], tile_src[None, :], tiles,
                )
            )
        )
        weight = jax.ShapeDtypeStruct((width, full), BF16)
        return pl.pallas_call(
            write_out,
            out_shape=shapes[:2] + (weight, weight),
            in_specs=[vmem] * 3,
            out_specs=(stay,) * 4,
            scratch_shapes=[pltpu.SemaphoreType.DMA((4,))],
        )(*(pltpu.with_memory_space_constraint(v, pltpu.VMEM) for v in results))

    in_specs = (
        P("dom", "rep"),
        P("rep", None),
        P("rep", None),
        P("dom", "rep"),
        P("dom", None),
        P("dom"),
        P("dom"),
        P("dom"),
        P("dom", None, None),
    )
    out_specs = (P("dom", "rep"), P("dom", "rep"), P("rep", None), P("rep", None))
    return jax.shard_map(local, mesh=mesh, in_specs=in_specs, out_specs=out_specs, check_vma=False)
```

```python
import functools

import jax
import jax.numpy as jnp
from jax import lax
from jax.experimental import pallas as pl
from jax.experimental.pallas import tpu as pltpu
from jax.sharding import PartitionSpec as P

MESH = pl.DeviceIdType.MESH
F32 = jnp.float32
BF16 = jnp.bfloat16
CORES = 2
GRIDS = {128: (8, 8), 8: (2, 2)}

NN = (((1,), (0,)), ((), ()))
TN = (((0,), (0,)), ((), ()))
NT = (((1,), (1,)), ((), ()))


def dot(a, b, dims=NN):
    return lax.dot_general(a, b, dims, preferred_element_type=F32)


def far_first(n):
    return sorted(range(1, n), key=lambda k: -min(k, n - k))


class Exchange:
    def __init__(self, n, me, device, src, dst, send_sem, recv_sem):
        self.n, self.me, self.device = n, me, device
        self.src, self.dst = src, dst
        self.send_sem, self.recv_sem = send_sem, recv_sem

    def copy(self, k, src, dst, peer):
        return pltpu.make_async_remote_copy(
            src_ref=src,
            dst_ref=dst,
            send_sem=self.send_sem.at[k - 1],
            recv_sem=self.recv_sem.at[k - 1],
            device_id=self.device(peer),
            device_id_type=MESH,
        )

    def each(self, step):
        for k in reversed(far_first(self.n)):
            step(k)

    def outgoing(self, k):
        peer = lax.rem(self.me + k, self.n)
        return self.copy(k, self.src(peer), self.dst(self.me, k), peer)

    def start(self):
        for k in far_first(self.n):
            self.outgoing(k).start()

    def wait_send(self):
        self.each(lambda k: self.outgoing(k).wait_send())

    def wait_recv_one(self, k):
        peer = lax.rem(self.me - k + self.n, self.n)
        slot = self.dst(peer, k)
        self.copy(k, slot, slot, peer).wait_recv()

    def wait_recv(self):
        self.each(self.wait_recv_one)


def kernel(
    dims,
    feat_in, w_self_in, w_neigh_in, grad_out_in, list_in, count_in, dst_in, src_in, tiles_in,
    hidden, grad_feat, out_w,
    weights, grad_out, list_t, count, tile_dst, tile_src, tiles,
    perm01, perm10, hot0, hot1, edges, edges_t, degree, own_sum,
    o0, a0, s0, b0, o1, a1, s1, b1,
    acts, acts_peer, w_cols, pre_act, grads, grads_peer, direct, grad_agg,
    c0, d0, e0, f0, c1, d1, e1, f1,
    w_acc, wa_send, wa_recv, wb_send, wb_recv, wt_send,
    in_sem,
    sem_a0, sem_a1, sem_b0, sem_b1, sem_feat, sem_cols, sem_cols_core, sem_agg, sem_acts,
    sem_gather, sem_pass, sem_d0, sem_d1, sem_f0, sem_f1, sem_first, sem_second,
    sem_third, sem_fourth, sem_swap,
):
    ny, nz, nx = dims
    ng = nz * CORES
    nd = ny * ng
    rows, width = feat_in.shape
    half = width // 2
    slots = list_in.shape[0]
    entries = nd * slots
    tile_count, tile_rows = tiles_in.shape[0], tiles_in.shape[1]
    dst_count = rows // tile_rows
    src_count = (rows + entries) // tile_rows
    parts = nz // nx
    band, piece = half // ny, width // parts

    dom = lax.axis_index("dom")
    x = lax.axis_index("rep")
    y = lax.div(dom, ng)
    g = lax.rem(dom, ng)
    z = lax.div(g, CORES)
    c = lax.rem(g, CORES)

    def at_g(peer):
        return (y * ng + peer, x)

    def at_y(peer):
        return (peer * ng + g, x)

    def at_z(peer):
        return (y * ng + peer * CORES + c, x)

    def at_c(peer):
        return (y * ng + z * CORES + peer, x)

    def at_x(peer):
        return (dom, peer)

    def fetch(i, src, dst):
        return pltpu.make_async_copy(src, dst, in_sem.at[i])

    fetches = [
        fetch(0, list_in, list_t),
        fetch(1, count_in, count),
        fetch(2, feat_in, acts.at[0, x]),
        fetch(3, w_self_in, weights.at[0]),
        fetch(4, w_neigh_in, weights.at[1]),
        fetch(5, dst_in, tile_dst),
        fetch(6, src_in, tile_src),
        fetch(7, tiles_in, tiles),
        fetch(8, grad_out_in, grad_out),
    ]
    barrier = pltpu.get_barrier_semaphore()

    def greet_one(device):
        pl.semaphore_signal(barrier, inc=1, device_id=device, device_id_type=MESH)

    def greet(n, me, device):
        for k in far_first(n):
            greet_one(device(lax.rem(me + k, n)))

    greet(ny, y, at_y)
    greet(ng, g, at_g)
    greet(nx, x, at_x)

    ways = (dict(n=ny, me=y, at=at_y), dict(n=nz, me=z, at=at_z))

    def across(h, i, column):
        return (ways[1 - h]["at"](i)[0], column)

    def senders(h, step):
        def one(k):
            i, column = x * parts + k // nx, k % nx

            @pl.when(jnp.logical_or(i != ways[1 - h]["me"], column != x))
            def _():
                step(k, i, column)

        for k in range(parts * nx):
            one(k)

    expected = (ng - 1) + (ny - 1) + (nx - 1)
    for f in fetches:
        f.start()

    def iota(shape, axis):
        return lax.broadcasted_iota(jnp.int32, shape, axis)

    col = iota((1, entries), 1)
    row = iota((entries, entries), 0)

    def selection(index):
        return jnp.where(row == index, 1.0, 0.0).astype(BF16)

    from_listed = selection(lax.rem(col, slots) * nd + lax.div(col, slots))
    y_in = lax.rem(lax.div(col, slots), ny)
    g_in = lax.div(col, slots * ny)
    slot_in = lax.rem(col, slots)
    perm01[...] = selection((y_in * ng + g_in) * slots + slot_in)

    fetches[0].wait()
    fetches[1].wait()
    listed = jnp.concatenate(
        [jnp.where(j < count[...], list_t[j : j + 1, :], -1) for j in range(slots)], axis=1
    )
    listed = jnp.broadcast_to(listed.astype(F32), (8, entries)).astype(BF16)
    natural = dot(listed, from_listed)
    transposed = dot(natural.astype(BF16), perm01[...])
    vertex = iota((rows, entries), 0).astype(F32)
    hot0[...] = jnp.where(vertex == transposed[0:1, :], 1.0, 0.0).astype(BF16)
    hot1[...] = jnp.where(vertex == natural[0:1, :], 1.0, 0.0).astype(BF16)
    per_g, per_y = entries // ng, entries // ny
    fetches[2].wait()
    feat = acts[0, x]
    o0[...] = dot(hot0[...], feat[:, :half], TN).astype(BF16).reshape(ng, per_g, half)
    o1[...] = dot(hot1[...], feat[:, half:], TN).astype(BF16).reshape(ny, per_y, half)

    pl.semaphore_wait(barrier, expected)

    out_a0 = Exchange(ng, g, at_g, lambda p: o0.at[p], lambda s, k: a0.at[s], *sem_pair(sem_a0))
    out_a1 = Exchange(ny, y, at_y, lambda p: o1.at[p], lambda s, k: a1.at[s], *sem_pair(sem_a1))
    out_b0 = Exchange(ny, y, at_y, lambda p: s0.at[p], lambda s, k: b0.at[s], *sem_pair(sem_b0))
    out_b1 = Exchange(ng, g, at_g, lambda p: s1.at[p], lambda s, k: b1.at[s], *sem_pair(sem_b1))
    out_a0.start()
    out_a1.start()

    def columns(p):
        return pl.ds(pl.multiple_of(p * width, width), width)

    feats = Exchange(
        nx, x, at_x, lambda p: acts.at[0, x], lambda s, k: acts.at[0, s], *sem_pair(sem_feat)
    )
    cols = Exchange(
        nx, x, at_x, lambda p: weights.at[c, :, columns(p)], lambda s, k: w_cols.at[c, s],
        *sem_pair(sem_cols)
    )
    cols_core = Exchange(
        CORES, c, at_c, lambda p: w_cols.at[c], lambda s, k: w_cols.at[s], *sem_pair(sem_cols_core)
    )
    fetches[3].wait()
    fetches[4].wait()
    cols.start()
    feats.start()
    a0[g] = o0[g]
    a1[y] = o1[y]
    w_cols[c, x] = weights[c, :, columns(x)]

    y_out = lax.div(col, slots * ng)
    g_out = lax.rem(lax.div(col, slots), ng)
    perm10[...] = selection((g_out * ny + y_out) * slots + slot_in)
    for f in fetches[5:]:
        f.wait()

    out_a1.wait_recv()
    s1[...] = dot(perm10[...], a1[...].reshape(entries, half)).astype(BF16).reshape(ng, per_g, half)
    out_b1.start()
    out_a0.wait_recv()
    s0[...] = dot(perm01[...], a0[...].reshape(entries, half)).astype(BF16).reshape(ny, per_y, half)
    out_b0.start()
    b0[y] = s0[y]
    b1[g] = s1[g]

    block_of = tile_dst[...] * src_count + tile_src[...]
    for i in range(dst_count):
        for j in range(src_count):
            here = jnp.where(block_of == i * src_count + j, 1.0, 0.0)
            total = jnp.zeros((tile_rows, tile_rows), F32)
            for t in range(tile_count):
                total += here[:, t : t + 1] * tiles[t].astype(F32)
            top = total.astype(BF16)
            at = (pl.ds(i * tile_rows, tile_rows), pl.ds(j * tile_rows, tile_rows))
            edges[(0,) + at] = top
            edges[(1,) + at] = (total - top.astype(F32)).astype(BF16)
    ones = jnp.ones((rows + entries, tile_rows), BF16)
    degree[...] = jnp.maximum(dot(edges[0], ones) + dot(edges[1], ones), 1.0)
    for i in range(2):
        edges_t[i] = dot(edges[i, :, rows:], perm01[...]).astype(BF16)
    own_sum[...] = dot(edges[0, :, :rows], feat) + dot(edges[1, :, :rows], feat)
    cols.wait_recv()
    cols_core.start()

    safe = jnp.concatenate([degree[...]] * (width // tile_rows), axis=1)
    def gather_mean(h):
        here = pl.ds(h * half, half)
        return Exchange(
            nx, x, at_x, lambda p: acts.at[1, x, :, here], lambda s, k: acts.at[1, s, :, here],
            *sem_pair(sem_agg, h)
        )

    aggs = [gather_mean(0), gather_mean(1)]
    out_b0.wait_recv()
    mirrored = b0[...].reshape(entries, half)
    left = dot(edges[0, :, rows:], mirrored) + dot(edges[1, :, rows:], mirrored)
    acts[1, x, :, :half] = ((own_sum[:, :half] + left) / safe[:, :half]).astype(BF16)
    aggs[0].start()
    out_b1.wait_recv()
    mirrored = b1[...].reshape(entries, half)
    right = dot(edges_t[0], mirrored) + dot(edges_t[1], mirrored)
    acts[1, x, :, half:] = ((own_sum[:, half:] + right) / safe[:, half:]).astype(BF16)
    aggs[1].start()

    def pass_acts(k):
        q = lax.rem(x - k + nx, nx)
        return Exchange(
            CORES, c, at_c, lambda p: acts.at[p, q], lambda s, i: acts_peer.at[q],
            *(sem.at[pl.ds(k, 1)] for sem in sem_pair(sem_acts))
        )

    feats.wait_recv()
    send_acts = [pass_acts(k) for k in range(nx)]
    send_acts[0].start()
    cols_core.wait_recv()
    total = dot(acts[1, x], w_cols[1, x])
    for q in range(nx):
        total += dot(acts[0, q], w_cols[0, q])
    pre_act[...] = total
    for k in range(1, nx):
        q = lax.rem(x - k + nx, nx)
        aggs[0].wait_recv_one(k)
        aggs[1].wait_recv_one(k)
        send_acts[k].start()
        pre_act[...] += dot(acts[1, q], w_cols[1, q])
    value = pre_act[...]
    sig = jax.nn.sigmoid(value)
    grads[x] = (grad_out[...].astype(F32) * (sig + value * sig * (1.0 - sig))).astype(BF16)

    send_grads = Exchange(
        CORES, c, at_c, lambda p: grads.at[x], lambda s, k: grads_peer, *sem_pair(sem_pass)
    )
    gather = Exchange(
        nx, x, at_x, lambda p: grads.at[x], lambda s, k: grads.at[s], *sem_pair(sem_gather)
    )
    send_grads.start()
    gather.start()
    hidden[...] = (value * sig).astype(BF16)

    for q in range(nx):
        w_acc[q] = dot(acts[c, q], grads[x], TN)
    for done in send_acts:
        done.wait_recv()
    send_grads.wait_recv()
    for q in range(nx):
        block = (w_acc[q] + dot(acts_peer[q], grads_peer[...], TN)).astype(BF16)
        for h in range(2):
            wa_send[h, :, q] = block[h * half : (h + 1) * half, :].reshape(ny, band, width)

    def first(h):
        way = ways[h]
        return Exchange(
            way["n"], way["me"], way["at"], lambda p: wa_send.at[h, p],
            lambda s, k: wa_recv.at[h, k - 1], *sem_pair(sem_first, h)
        )

    firsts = [first(0), first(1)]
    for way in firsts:
        way.start()

    direct[...] = dot(grads[x], weights[0, :, columns(x)], NT)
    grad_agg[...] = dot(grads[x], weights[1, :, columns(x)], NT)
    for k in range(1, nx):
        q = lax.rem(x - k + nx, nx)
        gather.wait_recv_one(k)
        direct[...] += dot(grads[q], weights[0, :, columns(q)], NT)
        grad_agg[...] += dot(grads[q], weights[1, :, columns(q)], NT)
    scaled = (grad_agg[...] / safe).astype(BF16)
    left, right = scaled[:, :half], scaled[:, half:]
    left = dot(edges[0, :, rows:], left, TN) + dot(edges[1, :, rows:], left, TN)
    right = dot(edges_t[0], right, TN) + dot(edges_t[1], right, TN)
    c0[...] = left.astype(BF16).reshape(ny, per_y, half)
    c1[...] = right.astype(BF16).reshape(ng, per_g, half)
    back_d0 = Exchange(ny, y, at_y, lambda p: c0.at[p], lambda s, k: d0.at[s], *sem_pair(sem_d0))
    back_d1 = Exchange(ng, g, at_g, lambda p: c1.at[p], lambda s, k: d1.at[s], *sem_pair(sem_d1))
    back_f0 = Exchange(ng, g, at_g, lambda p: e0.at[p], lambda s, k: f0.at[s], *sem_pair(sem_f0))
    back_f1 = Exchange(ny, y, at_y, lambda p: e1.at[p], lambda s, k: f1.at[s], *sem_pair(sem_f1))
    back_d0.start()
    back_d1.start()
    d0[y] = c0[y]
    d1[g] = c1[g]

    def second(h):
        way = ways[1 - h]
        return Exchange(
            way["n"], way["me"], way["at"], lambda p: wb_send.at[h, p],
            lambda s, k: wb_recv.at[h, k - 1], *sem_pair(sem_second, h)
        )

    seconds = [second(0), second(1)]
    for h in range(2):
        firsts[h].wait_recv()
        way, after = ways[h], ways[1 - h]
        for q in range(nx):
            total = wa_send[h, way["me"], q].astype(F32)
            for k in range(way["n"] - 1):
                total = total + wa_recv[h, k, q].astype(F32)
            for i in range(parts):
                wb_send[h, q * parts + i] = total[:, i * piece : (i + 1) * piece]
        seconds[h].start()

    direct[...] += dot(edges[0, :, :rows], scaled, TN) + dot(edges[1, :, :rows], scaled, TN)

    scale = float(rows * nd) ** (-0.5)

    def piece_at(h, i, column):
        r = h * half + ways[h]["me"] * band
        q = column * width + lax.rem(i, parts) * piece
        return out_w.at[c, pl.ds(pl.multiple_of(r, band), band), pl.ds(pl.multiple_of(q, piece), piece)]

    def third(h, k, dst, device, slot):
        return pltpu.make_async_remote_copy(
            src_ref=wt_send.at[h], dst_ref=dst, send_sem=sem_third.at[h, 0, k],
            recv_sem=sem_third.at[h, 1, slot], device_id=device, device_id_type=MESH,
        )

    def thirds(h, step):
        after = ways[1 - h]
        me = after["me"]
        slot = lax.rem(me, parts) * nx + x
        target = lax.div(me, parts)

        def one(k):
            copy = third(h, k, piece_at(h, me, x), across(h, lax.rem(me + k, after["n"]), target), slot)

            if k != 0:
                step(copy)
            else:
                pl.when(target != x)(lambda: step(copy))

        for k in far_first(after["n"]) + [0]:
            one(k)

    for h in range(2):
        seconds[h].wait_recv()
        after = ways[1 - h]
        total = wb_send[h, after["me"]]
        for k in range(after["n"] - 1):
            total = total + wb_recv[h, k]
        wt_send[h] = (total * scale).astype(BF16)
        thirds(h, lambda copy: copy.start())

        @pl.when(lax.div(after["me"], parts) == x)
        def _():
            piece_at(h, after["me"], x)[...] = wt_send[h]

    back_d0.wait_recv()
    e0[...] = dot(perm10[...], d0[...].reshape(entries, half)).astype(BF16).reshape(ng, per_g, half)
    back_f0.start()
    back_d1.wait_recv()
    e1[...] = dot(perm01[...], d1[...].reshape(entries, half)).astype(BF16).reshape(ny, per_y, half)
    back_f1.start()
    f0[g] = e0[g]
    f1[y] = e1[y]

    def band_at(h, i, core):
        return out_w.at[core, pl.ds(pl.multiple_of(h * half + i * band, band), band), :]

    def fourth(h):
        way = ways[h]
        return Exchange(
            way["n"], way["me"], way["at"], lambda p: band_at(h, way["me"], c),
            lambda s, k: band_at(h, s, c), *sem_pair(sem_fourth, h)
        )

    def swap(h, k):
        way = ways[h]
        i = lax.rem(way["me"] - k + way["n"], way["n"])
        return pltpu.make_async_remote_copy(
            src_ref=band_at(h, i, c), dst_ref=band_at(h, i, c), send_sem=sem_swap.at[h, 0, k],
            recv_sem=sem_swap.at[h, 1, k], device_id=at_c(1 - c), device_id_type=MESH,
        )

    fourths = [fourth(0), fourth(1)]
    for h in range(2):
        senders(
            h,
            lambda k, i, column: third(h, 0, piece_at(h, i, column), across(h, i, column), k).wait_recv(),
        )
        fourths[h].start()
        swap(h, 0).start()

    for h in range(2):
        thirds(h, lambda copy: copy.wait_send())
    for done in (
        [out_a0, out_a1, out_b0, out_b1, feats, cols, cols_core, send_grads, gather]
        + [back_d0, back_d1] + aggs + send_acts + firsts + seconds
    ):
        done.wait_send()

    def pass_on(k):
        for h in range(2):
            fourths[h].wait_recv_one(k)
            swap(h, k).start()

    near = far_first(ny)[::-1]
    for k in near[: ny // 2]:
        pass_on(k)
    back_f0.wait_recv()
    grad_feat[:, :half] = (
        direct[:, :half] + dot(hot0[...], f0[...].reshape(entries, half))
    ).astype(BF16)
    back_f1.wait_recv()
    grad_feat[:, half:] = (
        direct[:, half:] + dot(hot1[...], f1[...].reshape(entries, half))
    ).astype(BF16)
    back_f0.wait_send()
    back_f1.wait_send()
    for k in near[ny // 2 :]:
        pass_on(k)
    for done in fourths:
        done.wait_send()
    for k in [0] + near:
        for h in range(2):
            swap(h, k).wait_send()
            swap(h, k).wait_recv()


def write_out(hidden, grad_feat, both, out0, out1, out2, out3, sem):
    pairs = ((hidden, out0), (grad_feat, out1), (both.at[0], out2), (both.at[1], out3))
    copies = [pltpu.make_async_copy(src, dst, sem.at[i]) for i, (src, dst) in enumerate(pairs)]
    for copy in copies:
        copy.start()
    for copy in copies:
        copy.wait()


def sem_pair(sems, use=0):
    return sems.at[use, 0], sems.at[use, 1]


def solution(mesh):
    doms, nx = mesh.shape["dom"], mesh.shape["rep"]
    ny, nz = GRIDS[doms]
    ng = nz * CORES

    def local(
        features, w_self, w_neigh, grad_out, mirror_list, mirror_count, tile_dst, tile_src, tiles
    ):
        rows, width = features.shape
        half, full = width // 2, width * nx
        slots = mirror_list.shape[1]
        entries = doms * slots
        tile_count, tile_rows = tiles.shape[0], tiles.shape[1]
        per_g, per_y = entries // ng, entries // ny
        assert ny == nz and rows == width and nz % nx == 0
        parts = nz // nx
        band, piece = half // ny, width // parts
        vmem, stay = (pl.BlockSpec(memory_space=s) for s in (pltpu.VMEM, pl.ANY))

        def scratch(*shape, kind=BF16):
            return pltpu.VMEM(shape, kind)

        def sems(n, uses=1):
            return pltpu.SemaphoreType.DMA((uses, 2, n))

        by_g, by_y = scratch(ng, per_g, half), scratch(ny, per_y, half)
        buffers = [
            scratch(2, width, full), scratch(rows, width),
            scratch(slots, doms, kind=jnp.int32), scratch(1, doms, kind=jnp.int32),
            scratch(1, tile_count, kind=jnp.int32), scratch(1, tile_count, kind=jnp.int32),
            scratch(tile_count, tile_rows, tile_rows),
            scratch(entries, entries), scratch(entries, entries),
            scratch(rows, entries), scratch(rows, entries),
            scratch(2, rows, rows + entries), scratch(2, rows, entries),
            scratch(rows, tile_rows, kind=F32),
            scratch(rows, width, kind=F32),
            by_g, by_g, by_y, by_y, by_y, by_y, by_g, by_g,
            scratch(2, nx, rows, width), scratch(nx, rows, width), scratch(2, nx, width, width),
            scratch(rows, width, kind=F32), scratch(nx, rows, width), scratch(rows, width),
            scratch(rows, width, kind=F32), scratch(rows, width, kind=F32),
            by_y, by_y, by_g, by_g, by_g, by_g, by_y, by_y,
            scratch(nx, width, width, kind=F32),
            scratch(2, ny, nx, band, width), scratch(2, ny - 1, nx, band, width),
            scratch(2, nz, band, piece, kind=F32), scratch(2, nz - 1, band, piece, kind=F32),
            scratch(2, band, piece),
        ]
        semaphores = [
            pltpu.SemaphoreType.DMA((9,)),
            sems(ng - 1), sems(ny - 1), sems(ny - 1), sems(ng - 1),
            sems(nx - 1), sems(nx - 1), sems(1), sems(nx - 1, 2), sems(nx),
            sems(nx - 1), sems(1), sems(ny - 1), sems(ng - 1), sems(ng - 1), sems(ny - 1),
            sems(ny - 1, 2), sems(ny - 1, 2), sems(nz, 2), sems(ny - 1, 2), sems(ny, 2),
        ]
        shapes = (
            jax.ShapeDtypeStruct((rows, width), BF16),
            jax.ShapeDtypeStruct((rows, width), BF16),
            jax.ShapeDtypeStruct((2, width, full), BF16),
        )
        results = pl.pallas_call(
            functools.partial(kernel, (ny, nz, nx)),
            out_shape=tuple(pltpu.VMEM(v.shape, v.dtype) for v in shapes),
            in_specs=[pl.BlockSpec(memory_space=pltpu.HBM)] * 9,
            out_specs=(vmem, vmem, vmem),
            scratch_shapes=buffers + semaphores,
            compiler_params=pltpu.CompilerParams(
                collective_id=0, has_side_effects=True, vmem_limit_bytes=32 * 2**20
            ),
        )(
            *(
                pltpu.with_memory_space_constraint(v, pltpu.HBM)
                for v in (
                    features, w_self, w_neigh, grad_out, mirror_list.T, mirror_count[None, :],
                    tile_dst[None, :], tile_src[None, :], tiles,
                )
            )
        )
        weight = jax.ShapeDtypeStruct((width, full), BF16)
        return pl.pallas_call(
            write_out,
            out_shape=shapes[:2] + (weight, weight),
            in_specs=[vmem] * 3,
            out_specs=(stay,) * 4,
            scratch_shapes=[pltpu.SemaphoreType.DMA((4,))],
        )(*(pltpu.with_memory_space_constraint(v, pltpu.VMEM) for v in results))

    in_specs = (
        P("dom", "rep"),
        P("rep", None),
        P("rep", None),
        P("dom", "rep"),
        P("dom", None),
        P("dom"),
        P("dom"),
        P("dom"),
        P("dom", None, None),
    )
    out_specs = (P("dom", "rep"), P("dom", "rep"), P("rep", None), P("rep", None))
    return jax.shard_map(local, mesh=mesh, in_specs=in_specs, out_specs=out_specs, check_vma=False)
```
